32 devices in a mesh: src: 16 (over z, y, core), tgt: 2 (over x).
Axes of the slice: x: 2, y: 2, z: 4, core: 2. Of those that a mesh axis runs over, the one named last changes fastest.
Arguments:
- src_emb: bfloat16 [8192, 1024], P('src', 'tgt'), may hold values from -16 to 16
- tgt_emb: bfloat16 [8192, 1024], P('tgt', 'src'), may hold values from -16 to 16
- src_ids: int32 [8192], P('src'), may hold values from 0 to 4095
- tgt_ids: int32 [8192], P('tgt'), may hold values from 0 to 4095
Outputs:
- margin: float32 [8192, 8192], P('src', 'tgt')
The draws below stay inside these ranges and needn't reach their ends.
All inputs are finite; a program needn't handle non-finite values.
Results may differ from the reference program's by a relative error of at most 0.004.
Values may be sent and summed in bfloat16 or wider, within the bound.
A program may use at most 64 MiB of HBM per device.

```python
import jax
import jax.numpy as jnp
from jax import lax

D = 1024
NEIGH = 4
NS = 8192
NT = 8192


def sentence_tables(key):
    group_rows = jax.random.normal(jax.random.fold_in(key, 11), (NT // 4, D), jnp.float32)
    ident_rows = jax.random.normal(jax.random.fold_in(key, 12), (NT // 2, D), jnp.float32)
    shared_part = jax.random.uniform(jax.random.fold_in(key, 13), (NT // 4,), jnp.float32, 0.1, 0.5)
    own_part = jax.random.uniform(jax.random.fold_in(key, 14), (NT // 2,), jnp.float32, 0.2, 0.45)
    return (group_rows, ident_rows, shared_part, own_part)


def draw_src_ids(key, part):
    return jax.random.randint(jax.random.fold_in(key, 21), (NS,), 0, NT // 2, dtype=jnp.int32)


def draw_tgt_ids(key, part):
    return jax.random.randint(jax.random.fold_in(key, 22), (NT,), 0, NT // 2, dtype=jnp.int32)


def mixed_rows(key, sentence_ids, salt):
    group_rows, ident_rows, shared_part, own_part = sentence_tables(key)
    count = sentence_ids.shape[0]
    group_ids = sentence_ids // 2
    shared_weight = jnp.take(shared_part, group_ids)
    own_weight = jnp.take(own_part, sentence_ids)
    rest_weight = 1.0 - shared_weight - own_weight
    noise_key = jax.random.fold_in(key, salt)
    noise = jax.random.normal(noise_key, (count, D), jnp.float32)
    rows = jnp.sqrt(shared_weight)[:, None] * jnp.take(group_rows, group_ids, axis=0)
    rows = rows + jnp.sqrt(own_weight)[:, None] * jnp.take(ident_rows, sentence_ids, axis=0)
    rows = rows + jnp.sqrt(rest_weight)[:, None] * noise
    return jnp.clip(rows, -16.0, 16.0).astype(jnp.bfloat16)


def draw_src_emb(key, part):
    return mixed_rows(key, draw_src_ids(key, part), 31)


def draw_tgt_emb(key, part):
    return mixed_rows(key, draw_tgt_ids(key, part), 32)


def setup_inputs(seed: int = 0) -> dict:
    keys = jax.random.split(jax.random.key(seed), 5)
    src_emb = draw_src_emb(jax.random.fold_in(keys[4], 71), 0)
    tgt_emb = draw_tgt_emb(jax.random.fold_in(keys[4], 71), 0)
    src_ids = draw_src_ids(jax.random.fold_in(keys[4], 71), 0)
    tgt_ids = draw_tgt_ids(jax.random.fold_in(keys[4], 71), 0)
    return dict(src_emb=src_emb, tgt_emb=tgt_emb, src_ids=src_ids, tgt_ids=tgt_ids)


epsilon = 1e-06
excluded_score = -2.0

def unit_rows(embedded):
    values = embedded.astype(jnp.float32)
    scale = jnp.sqrt(lax.optimization_barrier(jnp.sum(values * values, axis=1, keepdims=True)) + epsilon)
    return (values / scale).astype(jnp.bfloat16)

def best_four(values):
    return lax.top_k(values, NEIGH)[0]

def reference(src_emb, tgt_emb, src_ids, tgt_ids):
    src_unit = unit_rows(src_emb)
    tgt_unit = unit_rows(tgt_emb)
    block_rows = min(512, NS)
    blocks = NS // block_rows
    src_blocks = src_unit.reshape(blocks, block_rows, D)
    id_blocks = src_ids.reshape(blocks, block_rows)

    def cosines(rows, row_ids):
        scores = lax.dot_general(rows, tgt_unit, (((1,), (1,)), ((), ())), preferred_element_type=jnp.float32)
        same = row_ids[:, None] == tgt_ids[None, :]
        return (jnp.where(same, jnp.float32(excluded_score), scores), same)

    def first_pass(column_best, pieces):
        rows, row_ids = pieces
        scores, same = cosines(rows, row_ids)
        row_best = best_four(scores)
        merged = best_four(jnp.concatenate([column_best, best_four(scores.T)], axis=1))
        return (merged, row_best)
    start = jnp.full((NT, NEIGH), excluded_score, jnp.float32)
    column_best, row_best = lax.scan(first_pass, start, (src_blocks, id_blocks))
    knn_src = lax.optimization_barrier(jnp.mean(row_best, axis=-1))
    knn_tgt = lax.optimization_barrier(jnp.mean(column_best, axis=-1))

    def second_pass(pieces):
        rows, row_ids, row_knn = pieces
        scores, same = cosines(rows, row_ids)
        ratio = scores / (0.5 * (row_knn[:, None] + knn_tgt[None, :]))
        return jnp.where(same, jnp.float32(0.0), ratio)
    margin = lax.map(second_pass, (src_blocks, id_blocks, knn_src))
    return margin.reshape(NS, NT)
```

```python
import functools

import jax
import jax.numpy as jnp
from jax import lax
from jax.experimental import pallas as pl
from jax.experimental.pallas import tpu as pltpu
from jax.sharding import PartitionSpec as P

epsilon = 1e-06
excluded_score = -2.0
MESH = pl.DeviceIdType.MESH
CHUNK = 512
UNIT = 256
EVERY, EVERY_AT = 8, 7
Z_AHEAD = 4
Y_AHEAD = 6
BLOCK = 32
HOP = 1
Y_LAG = 1
CORE_LAG = 1
MERGE_LAG = 1


def sort4(v):
    a, b = jnp.maximum(v[0], v[1]), jnp.minimum(v[0], v[1])
    c, d = jnp.maximum(v[2], v[3]), jnp.minimum(v[2], v[3])
    top, e = jnp.maximum(a, c), jnp.minimum(a, c)
    f, low = jnp.maximum(b, d), jnp.minimum(b, d)
    return (top, jnp.maximum(e, f), jnp.minimum(e, f), low)


def merge(first, second):
    c = [jnp.maximum(first[k], second[3 - k]) for k in range(4)]
    a, b = jnp.maximum(c[0], c[2]), jnp.maximum(c[1], c[3])
    d, e = jnp.minimum(c[0], c[2]), jnp.minimum(c[1], c[3])
    return (jnp.maximum(a, b), jnp.minimum(a, b), jnp.maximum(d, e), jnp.minimum(d, e))


def insert(best, value):
    out = []
    for level in best[:-1]:
        out.append(jnp.maximum(level, value))
        value = jnp.minimum(level, value)
    out.append(jnp.maximum(best[-1], value))
    return tuple(out)


def absorb(best, values):
    whole = len(values) // 4 * 4
    for k in range(0, whole, 4):
        best = merge(best, sort4(values[k : k + 4]))
    for value in values[whole:]:
        best = insert(best, value)
    return best


def fold_sublanes(best, shifts=(4, 2, 1)):
    for shift in shifts:
        best = merge(best, tuple(pltpu.roll(level, shift, 0) for level in best))
    return best


def mean_of(best):
    return (best[0] + best[1] + best[2] + best[3]) * 0.25


def lowest(shape):
    return tuple(jnp.full(shape, -jnp.inf, jnp.float32) for _ in range(4))


def kernel(dims, x_ref, a_ref, sid_ref, tid_ref, s_out, kt_out, ks_out, sid, tid, sids, g, a_whole, a_unit, rowbest,
           colbuf, colin, tailin, ktown, rowbuf, rowin, zrecv, zsend, yrecv, ysend, crecv, csend, arecv, asend, rrecv,
           rsend, krecv, ksend, mrecv, msend, trecv, tsend, lsem):
    ns, nt, nz, chunks, cw, feats = dims
    s = lax.axis_index("src")
    t = lax.axis_index("tgt")
    z, y, c = s // 4, (s // 2) % 2, s % 2
    right = (s + 4, t)
    left = (s - 4, t)
    over = (z * 4 + (1 - y) * 2 + c, t)
    core = (s + 1 - 2 * c, t)
    rows, width = a_unit.shape
    part = a_ref.shape[1]
    per = cw // UNIT
    units = chunks * per
    split = units - per
    has_right, has_left = z + 1 < nz, z >= 1

    def remote(src, dst, send, recv, where):
        return pltpu.make_async_remote_copy(
            src_ref=src, dst_ref=dst, send_sem=send, recv_sem=recv, device_id=where, device_id_type=MESH
        )

    def chunk_cols(j):
        return pl.ds(pl.multiple_of(j * cw, cw), cw)

    barrier = pltpu.get_barrier_semaphore()

    @pl.when(has_right)
    def _():
        pl.semaphore_signal(barrier, inc=1, device_id=right, device_id_type=MESH)

    @pl.when(has_left)
    def _():
        pl.semaphore_signal(barrier, inc=1, device_id=left, device_id_type=MESH)

    pl.semaphore_signal(barrier, inc=1, device_id=over, device_id_type=MESH)
    pl.semaphore_signal(barrier, inc=1, device_id=core, device_id_type=MESH)
    for k in range(1, nt):
        pl.semaphore_signal(barrier, inc=1, device_id=(s, lax.rem(t + k, nt)), device_id_type=MESH)

    for j in range(chunks):
        pltpu.make_async_copy(x_ref.at[:, chunk_cols(j)], g.at[j, z, y, c], lsem.at[0]).start()
    acols = pl.ds(pl.multiple_of(t * part, part), part)
    local_a = pltpu.make_async_copy(a_ref, a_whole.at[:, acols], lsem.at[1])
    local_sid = pltpu.make_async_copy(sid_ref, sid, lsem.at[2])
    local_tid = pltpu.make_async_copy(tid_ref, tid, lsem.at[3])
    local_a.start()
    local_sid.start()
    local_tid.start()
    pl.semaphore_wait(barrier, 1 + nt + has_right.astype(jnp.int32) + has_left.astype(jnp.int32))

    firsts = [j for j in range(chunks) if j > 0 and j % EVERY == EVERY_AT]
    n_first, n_rest = len(firsts), chunks - len(firsts)

    def y_first(j):
        if isinstance(j, int):
            return j in firsts
        return jnp.logical_and(lax.rem(j, EVERY) == EVERY_AT, j > 0)

    def z_piece(j, zp, first):
        return g.at[j, zp, :, c] if first else g.at[j, zp, y, c]

    def to_right(j, zp, first, own=False):
        ref = z_piece(j, zp, first)
        src = x_ref.at[:, chunk_cols(j)] if own else ref
        return remote(src, ref, zsend.at[0, int(first), zp], zrecv.at[j, zp], right)

    def to_left(j, zp, first, own=False):
        ref = z_piece(j, zp, first)
        src = x_ref.at[:, chunk_cols(j)] if own else ref
        return remote(src, ref, zsend.at[1, int(first), zp], zrecv.at[j, zp], left)

    def to_over(j, zp, first, own=False):
        ref = g.at[j, zp, y, c]
        src = x_ref.at[:, chunk_cols(j)] if own else ref
        return remote(src, ref, ysend.at[int(first)], yrecv.at[j], over)

    def from_over(j, first):
        ref = g.at[j, z, 1 - y, c] if first else g.at[j, :, 1 - y, c]
        return remote(ref, ref, ysend.at[int(first)], yrecv.at[j], over)

    def to_core(j, yy):
        ref = g.at[j, :, yy, c]
        return remote(ref, ref, csend.at[0], crecv.at[j], core)

    def from_core(j):
        ref = g.at[j, :, :, 1 - c]
        return remote(ref, ref, csend.at[0], crecv.at[j], core)

    def start_side(j, first, to_side, there):
        @pl.when(there)
        def _():
            to_side(j, z, first, not first).start()

    def to_tgt(k):
        return remote(a_ref, a_whole.at[:, acols], asend.at[0], arecv.at[t], (s, lax.rem(t + k, nt)))

    z_ahead, y_ahead = min(Z_AHEAD, chunks), min(Y_AHEAD, chunks)
    depth = HOP * (nz - 1)
    for j in firsts:
        to_over(j, z, True, True).start()
    sides = ((to_left, has_left, HOP * z - depth), (to_right, has_right, -HOP * z))
    for j in range(max(y_ahead, z_ahead)):
        if j < y_ahead and j not in firsts:
            to_over(j, z, False, True).start()
        if j < z_ahead and j not in firsts:
            for to_side, there, lead in sides:
                start_side(j, False, to_side, jnp.logical_and(there, j < lead + z_ahead))
    for k in range(1, nt):
        to_tgt(k).start()
    pltpu.make_async_copy(g.at[:, z, y, c], g.at[:, z, y, c], lsem.at[0]).wait()
    for j in firsts:
        from_over(j, True).wait_recv()
        if j < z_ahead:
            for to_side, there, lead in sides:
                start_side(j, True, to_side, jnp.logical_and(there, j < lead + z_ahead))
    local_sid.wait()
    local_tid.wait()
    sids[...] = jnp.broadcast_to(sid[...], (128, rows)).T
    for k in range(4):
        rowbest[k] = jnp.full(rowbest.shape[1:], -jnp.inf, jnp.float32)

    def normalize_sources():
        local_a.wait()
        for k in range(1, nt):
            other = lax.rem(t + k, nt)
            cols = pl.ds(pl.multiple_of(other * part, part), part)
            remote(a_ref, a_whole.at[:, cols], asend.at[0], arecv.at[other], (s, other)).wait_recv()
        block = 16

        def step(r, carry):
            at = pl.ds(pl.multiple_of(r * block, block), block)
            v = a_whole[at, :].astype(jnp.float32)
            scale = jnp.sqrt(jnp.sum(v * v, axis=1, keepdims=True) + epsilon)
            a_unit[at, :] = (v / scale).astype(jnp.bfloat16)
            return carry

        lax.fori_loop(0, rows // block, step, 0, unroll=2)

    def compute(j):
        def squares(k, acc):
            v = g[j, k // 4, (k // 2) % 2, k % 2].astype(jnp.float32)
            return acc + jnp.sum((v * v).reshape(feats // 8, 8, cw), axis=0)

        acc = lax.fori_loop(0, ns, squares, jnp.zeros((8, cw), jnp.float32), unroll=2)
        inverse = jnp.broadcast_to(1.0 / jnp.sqrt(jnp.sum(acc, axis=0, keepdims=True) + epsilon), (8, cw))
        cols = chunk_cols(j)
        s_out[:, cols] = jnp.dot(a_unit[...], g[j].reshape(width, cw), preferred_element_type=jnp.float32)
        tids = jnp.broadcast_to(tid[:, cols], (8, cw))
        lanes = cw // 128

        def group(r, best):
            found = []
            for h in range(4):
                at = pl.ds(pl.multiple_of(r * 32 + h * 8, 8), 8)
                ids = sids[at, :]
                pieces = []
                for q in range(lanes):
                    span = slice(q * 128, (q + 1) * 128)
                    where = pl.ds(pl.multiple_of(j * cw + q * 128, 128), 128)
                    v = jnp.where(ids == tids[:, span], jnp.float32(excluded_score), s_out[at, where] * inverse[:, span])
                    s_out[at, where] = v
                    pieces.append(v)
                row = absorb(tuple(rowbest[k, at, :] for k in range(4)), pieces)
                for k in range(4):
                    rowbest[k, at, :] = row[k]
                found.append(pieces)
            return tuple(absorb(best[q], [found[h][q] for h in range(4)]) for q in range(lanes))

        best = lax.fori_loop(0, rows // 32, group, tuple(lowest((8, 128)) for _ in range(lanes)))
        row = lax.broadcasted_iota(jnp.int32, (8, 128), 0)
        for u in range(per):
            half = [fold_sublanes(best[u * (UNIT // 128) + q]) for q in range(UNIT // 128)]
            out = half[0][0]
            for q in range(2):
                for k in range(4):
                    out = jnp.where(row == q * 4 + k, half[q][k], out)
            colbuf[j * per + u] = out

    def col_copy(u, k):
        return remote(colbuf.at[u], colin.at[s], ksend.at[0], krecv.at[0], (u, t))

    def send_columns(j):
        for u in range(per):
            unit = j * per + u

            @pl.when(s != unit)
            def _():
                col_copy(unit, 0).start()

            @pl.when(s == unit)
            def _():
                colin[s] = colbuf[unit]

    def knn_of(pieces):
        best = absorb(lowest((8, 128)), pieces)
        return mean_of(fold_sublanes(best, (2, 1)))

    def mean_copy(k):
        return remote(ktown, kt_out.at[s], msend.at[0], mrecv.at[0], (lax.rem(s + k, ns), t))

    def merge_columns(j):
        @pl.when(s // per == j)
        def _():
            ref = colin.at[pl.ds(0, ns - 1)]
            remote(ref, ref, ksend.at[0], krecv.at[0], core).wait_recv()
            ktown[...] = knn_of([colin[p] for p in range(ns)])
            for k in range(1, ns):
                mean_copy(k).start()
            kt_out[s] = ktown[...]

    def within(j):
        return jnp.logical_and(j >= 0, j < chunks)

    def relay(to_side, there, behind_me, j, first):
        for d in range(nz - 1, 0, -1):
            zp, present = behind_me(d)

            @pl.when(present)
            def _():
                to_side(j, zp, first).wait_recv()

                @pl.when(there)
                def _():
                    to_side(j, zp, first).start()

                if not first:
                    to_over(j, zp, False).start()

    relays = (
        functools.partial(relay, to_left, has_left, lambda d: (z + d, z + d < nz)),
        functools.partial(relay, to_right, has_right, lambda d: (z - d, z - d >= 0)),
    )

    def pass_on(j, first):
        to_core(j, y).start()
        if first:
            to_core(j, 1 - y).start()

    y_behind = depth + Y_LAG
    behind = y_behind + CORE_LAG

    def either(j, what):
        @pl.when(jnp.logical_and(within(j), jnp.logical_not(y_first(j))))
        def _():
            what(j, False)

        if n_first:

            @pl.when(jnp.logical_and(within(j), y_first(j)))
            def _():
                what(j, True)

    def tick(i, carry):
        for (to_side, there, lead), relay_side in zip(sides, relays):
            j = i + lead
            either(j + z_ahead, lambda j, first: start_side(j, first, to_side, there))
            either(j, relay_side)

        j = i - depth + y_ahead

        @pl.when(jnp.logical_and(j >= y_ahead, jnp.logical_and(j < chunks, jnp.logical_not(y_first(j)))))
        def _():
            to_over(j, z, False, True).start()

        either(i - depth, pass_on)

        jy = i - y_behind

        @pl.when(jnp.logical_and(within(jy), jnp.logical_not(y_first(jy))))
        def _():
            from_over(jy, False).wait_recv()
            to_core(jy, 1 - y).start()

        jc = i - behind

        @pl.when(jc == 0)
        def _():
            normalize_sources()

        @pl.when(jc >= 0)
        def _():
            from_core(jc).wait_recv()
            compute(jc)


        @pl.when(jnp.logical_and(jc >= 0, jc < chunks - 1))
        def _():
            send_columns(jc)

        @pl.when(jnp.logical_and(jc >= MERGE_LAG, jc < chunks - 1))
        def _():
            merge_columns(jc - MERGE_LAG)

        return carry

    lax.fori_loop(0, chunks + behind, tick, 0)

    def tail_copy(k):
        mine = tailin.at[s]
        return remote(colbuf.at[pl.ds(split, per)], mine, tsend.at[0], trecv.at[0], (lax.rem(s + k, ns), t))

    def row_copy(k):
        return remote(rowbuf, rowin.at[t], rsend.at[0], rrecv.at[0], (s, lax.rem(t + k, nt)))

    for k in range(1, ns):
        tail_copy(k).start()
    tailin[s] = colbuf[pl.ds(split, per)]
    for j in range(max(0, chunks - 1 - MERGE_LAG), chunks - 1):
        merge_columns(j)
    flat = [rowbest[k].T for k in range(4)]
    best = lowest((8, rows))
    for q in range(128 // 8):
        best = merge(best, tuple(flat[k][q * 8 : (q + 1) * 8, :] for k in range(4)))
    best = fold_sublanes(best)
    row = lax.broadcasted_iota(jnp.int32, (8, rows), 0)
    out = jnp.full((8, rows), -jnp.inf, jnp.float32)
    for k in range(4):
        out = jnp.where(row == k, best[k], out)
    rowbuf[...] = out
    rowin[t] = out
    for k in range(1, nt):
        row_copy(k).start()

    def drain_z(zp, first, count):
        ref = g.at[pl.ds(0, count), 0, :, 0] if first else g.at[pl.ds(0, count), 0, 0, 0]

        @pl.when(jnp.logical_and(has_right, zp <= z))
        def _():
            remote(ref, ref, zsend.at[0, int(first), zp], zrecv.at[0, zp], right).wait_send()

        @pl.when(jnp.logical_and(has_left, zp >= z))
        def _():
            remote(ref, ref, zsend.at[1, int(first), zp], zrecv.at[0, zp], left).wait_send()

    for zp in range(nz):
        drain_z(zp, False, n_rest)
        if n_first:
            drain_z(zp, True, n_first)
    ref = g.at[pl.ds(0, n_rest), :, 0, 0]
    remote(ref, ref, ysend.at[0], yrecv.at[0], over).wait_send()
    if n_first:
        ref = g.at[pl.ds(0, n_first), 0, 0, 0]
        remote(ref, ref, ysend.at[1], yrecv.at[0], over).wait_send()
    ref = g.at[:, :, :, c]
    remote(ref, ref, csend.at[0], crecv.at[0], core).wait_send()
    for k in range(1, nt):
        to_tgt(k).wait_send()

    ref = tailin.at[pl.ds(0, ns - 1)]
    remote(ref, ref, tsend.at[0], trecv.at[0], core).wait_recv()
    for u in range(per):
        kt_out[split + u] = knn_of([tailin[p, u] for p in range(ns)])
    for k in range(1, nt):
        row_copy(k).wait_send()
    ref = rowin.at[pl.ds(0, nt - 1)]
    remote(ref, ref, rsend.at[0], rrecv.at[0], core).wait_recv()
    half = 0.5 * mean_of(fold_sublanes(absorb(lowest((8, rows)), [rowin[p] for p in range(nt)])))
    ks_out[...] = jnp.broadcast_to(half[0:1], (128, rows)).T

    @pl.when(s < split)
    def _():
        ref = colbuf.at[pl.ds(0, split - 1)]
        remote(ref, ref, ksend.at[0], krecv.at[0], core).wait_send()
        mean = kt_out.at[pl.ds(0, split - 1)]
        remote(mean, mean, msend.at[0], mrecv.at[0], core).wait_recv()
        for k in range(1, ns):
            mean_copy(k).wait_send()

    @pl.when(s >= split)
    def _():
        ref = colbuf.at[pl.ds(0, split)]
        remote(ref, ref, ksend.at[0], krecv.at[0], core).wait_send()
        mean = kt_out.at[pl.ds(0, split)]
        remote(mean, mean, msend.at[0], mrecv.at[0], core).wait_recv()

    ref = tailin.at[pl.ds(0, ns - 1)]
    remote(ref, ref, tsend.at[0], trecv.at[0], core).wait_send()


def finish(s_ref, kt_ref, ks_ref, out_ref, half, held, sem):
    rows, cols = s_ref.shape
    tiles = cols // 128
    for u in range(tiles // 2):
        for q in range(2):
            half[2 * u + q] = jnp.broadcast_to(0.5 * kt_ref[u, 4 * q + 3 : 4 * q + 4, :], (8, 128))

    def block(b, carry):
        def at(h):
            return pl.ds(pl.multiple_of(b * BLOCK + 8 * h, 8), 8)

        mine = [ks_ref[at(h), :] for h in range(BLOCK // 8)]

        def tile(q, carry):
            lanes = pl.ds(pl.multiple_of(q * 128, 128), 128)
            other = half[q]
            for h in range(BLOCK // 8):
                v = s_ref[at(h), lanes]
                held[at(h), lanes] = jnp.where(v == excluded_score, jnp.float32(0.0), v / (mine[h] + other))
            return carry

        lax.fori_loop(0, tiles, tile, 0, unroll=4)
        span = pl.ds(pl.multiple_of(b * BLOCK, BLOCK), BLOCK)
        pltpu.make_async_copy(held.at[span], out_ref.at[span], sem.at[0]).start()
        return carry

    lax.fori_loop(0, rows // BLOCK, block, 0)
    pltpu.make_async_copy(held, out_ref, sem.at[0]).wait()


def body(ns, nt, src_emb, tgt_emb, src_ids, tgt_ids):
    rows, part = src_emb.shape
    cols, feats = tgt_emb.shape
    width = part * nt
    nz = ns // 4
    cw = min(CHUNK, cols)
    chunks = cols // cw
    units = cols // UNIT
    f32, bf16 = jnp.float32, jnp.bfloat16
    dma = pltpu.SemaphoreType.DMA
    hbm = pl.BlockSpec(memory_space=pltpu.MemorySpace.HBM)
    vmem = pl.BlockSpec(memory_space=pltpu.VMEM)
    args = (tgt_emb.T, src_emb, src_ids.reshape(1, rows), tgt_ids.reshape(1, cols))
    scores, kt, ks = pl.pallas_call(
        functools.partial(kernel, (ns, nt, nz, chunks, cw, feats)),
        out_shape=(
            jax.ShapeDtypeStruct((rows, cols), f32),
            jax.ShapeDtypeStruct((units, 8, 128), f32),
            jax.ShapeDtypeStruct((rows, 128), f32),
        ),
        in_specs=[hbm, hbm, hbm, hbm],
        out_specs=(vmem, vmem, vmem),
        scratch_shapes=[
            pltpu.VMEM((1, rows), jnp.int32),
            pltpu.VMEM((1, cols), jnp.int32),
            pltpu.VMEM((rows, 128), jnp.int32),
            pltpu.VMEM((chunks, nz, 2, 2, feats, cw), bf16),
            pltpu.VMEM((rows, width), bf16),
            pltpu.VMEM((rows, width), bf16),
            pltpu.VMEM((4, rows, 128), f32),
            pltpu.VMEM((units, 8, 128), f32),
            pltpu.VMEM((ns, 8, 128), f32),
            pltpu.VMEM((ns, cw // UNIT, 8, 128), f32),
            pltpu.VMEM((8, 128), f32),
            pltpu.VMEM((8, rows), f32),
            pltpu.VMEM((nt, 8, rows), f32),
            dma((chunks, nz)),
            dma((2, 2, nz)),
            dma((chunks,)),
            dma((2,)),
            dma((chunks,)),
            dma((1,)),
            dma((nt,)),
            dma((1,)),
            dma((1,)),
            dma((1,)),
            dma((1,)),
            dma((1,)),
            dma((1,)),
            dma((1,)),
            dma((1,)),
            dma((1,)),
            dma((4,)),
        ],
        compiler_params=pltpu.CompilerParams(
            collective_id=0, has_side_effects=True, vmem_limit_bytes=40 * 2**20
        ),
    )(*(pltpu.with_memory_space_constraint(v, pltpu.MemorySpace.HBM) for v in args))
    return pl.pallas_call(
        finish,
        out_shape=jax.ShapeDtypeStruct((rows, cols), f32),
        in_specs=[vmem, vmem, vmem],
        out_specs=pl.BlockSpec(memory_space=pl.ANY),
        scratch_shapes=[
            pltpu.VMEM((cols // 128, 8, 128), f32),
            pltpu.VMEM((rows, cols), f32),
            dma((1,)),
        ],
        compiler_params=pltpu.CompilerParams(vmem_limit_bytes=40 * 2**20),
    )(scores, kt, ks)


def solution(mesh):
    return jax.shard_map(
        functools.partial(body, mesh.shape["src"], mesh.shape["tgt"]),
        mesh=mesh,
        in_specs=(P("src", "tgt"), P("tgt", "src"), P("src"), P("tgt")),
        out_specs=P("src", "tgt"),
        check_vma=False,
    )
```

```python
import functools

import jax
import jax.numpy as jnp
from jax import lax
from jax.experimental import pallas as pl
from jax.experimental.pallas import tpu as pltpu
from jax.sharding import PartitionSpec as P

epsilon = 1e-06
excluded_score = -2.0
MESH = pl.DeviceIdType.MESH
CHUNK = 512
SWAP = False
Z_AHEAD = 3
Y_AHEAD = 7
BLOCK = 32
HOP = 1
Y_LAG = 2
CORE_LAG = 1


def sort4(v):
    a, b = jnp.maximum(v[0], v[1]), jnp.minimum(v[0], v[1])
    c, d = jnp.maximum(v[2], v[3]), jnp.minimum(v[2], v[3])
    top, e = jnp.maximum(a, c), jnp.minimum(a, c)
    f, low = jnp.maximum(b, d), jnp.minimum(b, d)
    return (top, jnp.maximum(e, f), jnp.minimum(e, f), low)


def merge(first, second):
    c = [jnp.maximum(first[k], second[3 - k]) for k in range(4)]
    a, b = jnp.maximum(c[0], c[2]), jnp.maximum(c[1], c[3])
    d, e = jnp.minimum(c[0], c[2]), jnp.minimum(c[1], c[3])
    return (jnp.maximum(a, b), jnp.minimum(a, b), jnp.maximum(d, e), jnp.minimum(d, e))


def insert(best, value):
    out = []
    for level in best[:-1]:
        out.append(jnp.maximum(level, value))
        value = jnp.minimum(level, value)
    out.append(jnp.maximum(best[-1], value))
    return tuple(out)


def absorb(best, values):
    whole = len(values) // 4 * 4
    for k in range(0, whole, 4):
        best = merge(best, sort4(values[k : k + 4]))
    for value in values[whole:]:
        best = insert(best, value)
    return best


def fold_sublanes(best, shifts=(4, 2, 1)):
    for shift in shifts:
        best = merge(best, tuple(pltpu.roll(level, shift, 0) for level in best))
    return best


def mean_of(best):
    return (best[0] + best[1] + best[2] + best[3]) * 0.25


def lowest(shape):
    return tuple(jnp.full(shape, -jnp.inf, jnp.float32) for _ in range(4))


def kernel(dims, x_ref, a_ref, sid_ref, tid_ref, s_out, kt_out, ks_out, sid, tid, sids, g, a_whole, a_unit, rowbest,
           colbuf, colin, tailin, ktown, rowbuf, rowin, zrecv, zsend, yrecv, ysend, crecv, csend, arecv, asend, rrecv,
           rsend, krecv, ksend, mrecv, msend, trecv, tsend, lsem):
    ns, nt, nz, chunks, cw, feats = dims
    s = lax.axis_index("src")
    t = lax.axis_index("tgt")
    z, y, c = s // 4, (s // 2) % 2, s % 2
    right = (s + 4, t)
    left = (s - 4, t)
    over = (z * 4 + (1 - y) * 2 + c, t)
    core = (s + 1 - 2 * c, t)
    rows, width = a_unit.shape
    part = a_ref.shape[1]
    lanes = cw // 128
    first = chunks - 1
    early, last = (first, first - 1) if SWAP else (first - 1, first)
    stride = ns // chunks
    has_right, has_left = z + 1 < nz, z >= 1

    def remote(src, dst, send, recv, where):
        return pltpu.make_async_remote_copy(
            src_ref=src, dst_ref=dst, send_sem=send, recv_sem=recv, device_id=where, device_id_type=MESH
        )

    def chunk_cols(j):
        return pl.ds(pl.multiple_of(j * cw, cw), cw)

    barrier = pltpu.get_barrier_semaphore()

    @pl.when(has_right)
    def _():
        pl.semaphore_signal(barrier, inc=1, device_id=right, device_id_type=MESH)

    @pl.when(has_left)
    def _():
        pl.semaphore_signal(barrier, inc=1, device_id=left, device_id_type=MESH)

    pl.semaphore_signal(barrier, inc=1, device_id=over, device_id_type=MESH)
    pl.semaphore_signal(barrier, inc=1, device_id=core, device_id_type=MESH)
    for k in range(1, nt):
        pl.semaphore_signal(barrier, inc=1, device_id=(s, lax.rem(t + k, nt)), device_id_type=MESH)

    for j in range(chunks):
        pltpu.make_async_copy(x_ref.at[:, chunk_cols(j)], g.at[j, z, y, c], lsem.at[0]).start()
    acols = pl.ds(pl.multiple_of(t * part, part), part)
    local_a = pltpu.make_async_copy(a_ref, a_whole.at[:, acols], lsem.at[1])
    local_sid = pltpu.make_async_copy(sid_ref, sid, lsem.at[2])
    local_tid = pltpu.make_async_copy(tid_ref, tid, lsem.at[3])
    local_a.start()
    local_sid.start()
    local_tid.start()
    pl.semaphore_wait(barrier, 1 + nt + has_right.astype(jnp.int32) + has_left.astype(jnp.int32))

    def to_right(j, zp, own=False):
        ref = g.at[j, zp, y, c]
        return remote(x_ref.at[:, chunk_cols(j)] if own else ref, ref, zsend.at[0, 0, zp], zrecv.at[j, zp], right)

    def to_left(j, zp, own=False):
        ref = g.at[j, zp, y, c]
        return remote(x_ref.at[:, chunk_cols(j)] if own else ref, ref, zsend.at[1, 0, zp], zrecv.at[j, zp], left)

    def both_right(zp):
        ref = g.at[first, zp, :, c]
        return remote(ref, ref, zsend.at[0, 1, zp], zrecv.at[first, zp], right)

    def both_left(zp):
        ref = g.at[first, zp, :, c]
        return remote(ref, ref, zsend.at[1, 1, zp], zrecv.at[first, zp], left)

    def to_over(j, zp, own=False):
        ref = g.at[j, zp, y, c]
        src = x_ref.at[:, chunk_cols(j)] if own else ref
        return remote(src, ref, ysend.at[0], yrecv.at[j], over)

    def from_over(j):
        ref = g.at[j, :, 1 - y, c]
        return remote(ref, ref, ysend.at[0], yrecv.at[j], over)

    def swap(own):
        ref = g.at[first, z, y, c] if own else g.at[first, z, 1 - y, c]
        return remote(x_ref.at[:, chunk_cols(first)] if own else ref, ref, ysend.at[1], yrecv.at[first], over)

    def to_core(j, yy):
        ref = g.at[j, :, yy, c]
        return remote(ref, ref, csend.at[0], crecv.at[j], core)

    def from_core(j):
        ref = g.at[j, :, :, 1 - c]
        return remote(ref, ref, csend.at[0], crecv.at[j], core)

    def to_tgt(k):
        return remote(a_ref, a_whole.at[:, acols], asend.at[0], arecv.at[t], (s, lax.rem(t + k, nt)))

    z_ahead, y_ahead = min(Z_AHEAD, first - 1), min(Y_AHEAD, first)
    depth = HOP * (nz - 1)
    sides = ((to_left, has_left, HOP * z - depth), (to_right, has_right, -HOP * z))
    swap(True).start()
    for j in range(max(y_ahead, z_ahead)):
        if j < y_ahead:
            to_over(j, z, True).start()
        if j < z_ahead:
            for to_side, there, lead in sides:

                @pl.when(jnp.logical_and(there, j < lead + z_ahead))
                def _():
                    to_side(j, z, True).start()

    for k in range(1, nt):
        to_tgt(k).start()
    pltpu.make_async_copy(g.at[:, z, y, c], g.at[:, z, y, c], lsem.at[0]).wait()
    swap(False).wait_recv()
    local_sid.wait()
    local_tid.wait()
    sids[...] = jnp.broadcast_to(sid[...], (128, rows)).T
    for k in range(4):
        rowbest[k] = jnp.full(rowbest.shape[1:], -jnp.inf, jnp.float32)

    def normalize_sources():
        local_a.wait()
        for k in range(1, nt):
            other = lax.rem(t + k, nt)
            cols = pl.ds(pl.multiple_of(other * part, part), part)
            remote(a_ref, a_whole.at[:, cols], asend.at[0], arecv.at[other], (s, other)).wait_recv()
        block = 16

        def step(r, carry):
            at = pl.ds(pl.multiple_of(r * block, block), block)
            v = a_whole[at, :].astype(jnp.float32)
            scale = jnp.sqrt(jnp.sum(v * v, axis=1, keepdims=True) + epsilon)
            a_unit[at, :] = (v / scale).astype(jnp.bfloat16)
            return carry

        lax.fori_loop(0, rows // block, step, 0, unroll=2)

    def compute(j):
        cols = chunk_cols(j)
        found = g[j].reshape(width, cw)
        s_out[:, cols] = jnp.dot(a_unit[...], found, preferred_element_type=jnp.float32)
        found = found.astype(jnp.float32)
        acc = jnp.sum((found * found).reshape(width // 8, 8, cw), axis=0)
        inverse = jnp.broadcast_to(1.0 / jnp.sqrt(jnp.sum(acc, axis=0, keepdims=True) + epsilon), (8, cw))
        tids = jnp.broadcast_to(tid[:, cols], (8, cw))

        def group(r, best):
            found = []
            for h in range(4):
                at = pl.ds(pl.multiple_of(r * 32 + h * 8, 8), 8)
                ids = sids[at, :]
                pieces = []
                for q in range(lanes):
                    span = slice(q * 128, (q + 1) * 128)
                    where = pl.ds(pl.multiple_of(j * cw + q * 128, 128), 128)
                    v = jnp.where(ids == tids[:, span], jnp.float32(excluded_score), s_out[at, where] * inverse[:, span])
                    s_out[at, where] = v
                    pieces.append(v)
                row = absorb(tuple(rowbest[k, at, :] for k in range(4)), pieces)
                for k in range(4):
                    rowbest[k, at, :] = row[k]
                found.append(pieces)
            return tuple(absorb(best[q], [found[h][q] for h in range(4)]) for q in range(lanes))

        best = lax.fori_loop(0, rows // 32, group, tuple(lowest((8, 128)) for _ in range(lanes)))
        best = [fold_sublanes(b) for b in best]
        row = lax.broadcasted_iota(jnp.int32, (8, 128), 0)
        tiles = []
        for q in range(0, lanes, 2):
            out = best[q][0]
            for k in range(1, 8):
                out = jnp.where(row == k, best[q + k // 4][k % 4], out)
            tiles.append(out)
        colbuf[j] = jnp.concatenate(tiles, axis=0).astype(jnp.bfloat16)

    def send_columns(j):
        owner = j * stride

        @pl.when(s != owner)
        def _():
            remote(colbuf.at[j], colin.at[s], ksend.at[0], krecv.at[0], (owner, t)).start()

        @pl.when(s == owner)
        def _():
            colin[s] = colbuf[j]

    def knn_of(ref):
        best = absorb(lowest((4 * lanes, 128)), [ref[p].astype(jnp.float32) for p in range(ns)])
        mean = mean_of(fold_sublanes(best, (2, 1)))
        return jnp.concatenate([mean[4 * q + 3 : 4 * q + 4] for q in range(lanes)], axis=0)

    def mean_copy(k):
        j = s // stride
        return remote(ktown, kt_out.at[j], msend.at[0], mrecv.at[0], (lax.rem(s + k, ns), t))

    def merge_columns(j):
        @pl.when(s == j * stride)
        def _():
            ref = colin.at[pl.ds(0, ns - 1)]
            remote(ref, ref, ksend.at[0], krecv.at[0], core).wait_recv()
            ktown[...] = knn_of(colin)
            for k in range(1, ns):
                mean_copy(k).start()
            kt_out[j] = ktown[...]

    def within(j):
        return jnp.logical_and(j >= 0, j < first)

    def relay(to_side, there, behind_me, j):
        for d in range(1, nz):
            zp, present = behind_me(d)

            @pl.when(present)
            def _():
                to_side(j, zp).wait_recv()

                @pl.when(there)
                def _():
                    to_side(j, zp).start()

                to_over(j, zp).start()

    relays = (
        functools.partial(relay, to_left, has_left, lambda d: (z + d, z + d < nz)),
        functools.partial(relay, to_right, has_right, lambda d: (z - d, z - d >= 0)),
    )

    def relay_both(both, there, behind_me):
        for d in range(1, nz):
            zp, present = behind_me(d)

            @pl.when(present)
            def _():
                both(zp).wait_recv()

                @pl.when(there)
                def _():
                    both(zp).start()

    relays_both = (
        functools.partial(relay_both, both_left, has_left, lambda d: (z + d, z + d < nz)),
        functools.partial(relay_both, both_right, has_right, lambda d: (z - d, z - d >= 0)),
    )

    y_behind = depth + Y_LAG
    behind = y_behind + CORE_LAG

    def tick(i, carry):
        for (to_side, there, lead), both, relay_side, relay_pair in zip(sides, (both_left, both_right), relays, relays_both):
            j = i + lead

            @pl.when(jnp.logical_and(j + z_ahead == first, there))
            def _():
                both(z).start()

            @pl.when(j == first)
            def _():
                relay_pair()

            @pl.when(jnp.logical_and(within(j + z_ahead), there))
            def _():
                to_side(j + z_ahead, z, True).start()

            @pl.when(within(j))
            def _():
                relay_side(j)

        j = i - depth

        @pl.when(jnp.logical_and(j >= 0, j + y_ahead < first))
        def _():
            to_over(j + y_ahead, z, True).start()

        @pl.when(within(j))
        def _():
            to_core(j, y).start()

        @pl.when(j == first)
        def _():
            to_core(first, y).start()
            to_core(first, 1 - y).start()

        jy = i - y_behind

        @pl.when(within(jy))
        def _():
            from_over(jy).wait_recv()
            to_core(jy, 1 - y).start()

        m = i - behind
        jc = jnp.where(m == first - 1, early, jnp.where(m == first, last, m))

        @pl.when(m == 0)
        def _():
            normalize_sources()

        @pl.when(m >= 0)
        def _():
            from_core(jc).wait_recv()
            compute(jc)


        @pl.when(jnp.logical_and(m >= 0, m < first))
        def _():
            send_columns(jc)

        @pl.when(jnp.logical_and(m >= 1, m < first))
        def _():
            merge_columns(m - 1)

        return carry

    lax.fori_loop(0, chunks + behind, tick, 0)

    def tail_copy(k):
        return remote(colbuf.at[last], tailin.at[s], tsend.at[0], trecv.at[0], (lax.rem(s + k, ns), t))

    def row_copy(k):
        return remote(rowbuf, rowin.at[t], rsend.at[0], rrecv.at[0], (s, lax.rem(t + k, nt)))

    for k in range(1, ns):
        tail_copy(k).start()
    tailin[s] = colbuf[last]
    merge_columns(early)
    flat = [rowbest[k].T for k in range(4)]
    best = lowest((8, rows))
    for q in range(128 // 8):
        best = merge(best, tuple(flat[k][q * 8 : (q + 1) * 8, :] for k in range(4)))
    best = fold_sublanes(best)
    row = lax.broadcasted_iota(jnp.int32, (8, rows), 0)
    out = jnp.full((8, rows), -jnp.inf, jnp.float32)
    for k in range(4):
        out = jnp.where(row == k, best[k], out)
    rowbuf[...] = out
    rowin[t] = out
    for k in range(1, nt):
        row_copy(k).start()

    def drain_z(zp, kind, ref):
        @pl.when(jnp.logical_and(has_right, zp <= z))
        def _():
            remote(ref, ref, zsend.at[0, kind, zp], zrecv.at[0, zp], right).wait_send()

        @pl.when(jnp.logical_and(has_left, zp >= z))
        def _():
            remote(ref, ref, zsend.at[1, kind, zp], zrecv.at[0, zp], left).wait_send()

    for zp in range(nz):
        drain_z(zp, 0, g.at[pl.ds(0, first), 0, 0, 0])
        drain_z(zp, 1, g.at[0, 0, :, 0])
    ref = g.at[pl.ds(0, first), :, 0, 0]
    remote(ref, ref, ysend.at[0], yrecv.at[0], over).wait_send()
    swap(True).wait_send()
    ref = g.at[:, :, :, c]
    remote(ref, ref, csend.at[0], crecv.at[0], core).wait_send()
    for k in range(1, nt):
        to_tgt(k).wait_send()

    ref = tailin.at[pl.ds(0, ns - 1)]
    remote(ref, ref, tsend.at[0], trecv.at[0], core).wait_recv()
    kt_out[last] = knn_of(tailin)
    for k in range(1, nt):
        row_copy(k).wait_send()
    ref = rowin.at[pl.ds(0, nt - 1)]
    remote(ref, ref, rsend.at[0], rrecv.at[0], core).wait_recv()
    half = 0.5 * mean_of(fold_sublanes(absorb(lowest((8, rows)), [rowin[p] for p in range(nt)])))
    ks_out[...] = jnp.broadcast_to(half[0:1], (128, rows)).T

    owns = jnp.logical_and(lax.rem(s, stride) == 0, s != last * stride)

    @pl.when(owns)
    def _():
        ref = colbuf.at[pl.ds(0, first - 1)]
        remote(ref, ref, ksend.at[0], krecv.at[0], core).wait_send()
        mean = kt_out.at[pl.ds(0, first - 1)]
        remote(mean, mean, msend.at[0], mrecv.at[0], core).wait_recv()
        for k in range(1, ns):
            mean_copy(k).wait_send()

    @pl.when(jnp.logical_not(owns))
    def _():
        ref = colbuf.at[pl.ds(0, first)]
        remote(ref, ref, ksend.at[0], krecv.at[0], core).wait_send()
        mean = kt_out.at[pl.ds(0, first)]
        remote(mean, mean, msend.at[0], mrecv.at[0], core).wait_recv()

    ref = tailin.at[pl.ds(0, ns - 1)]
    remote(ref, ref, tsend.at[0], trecv.at[0], core).wait_send()


def finish(s_ref, kt_ref, ks_ref, out_ref, half, held, sem):
    rows, cols = s_ref.shape
    tiles = cols // 128
    lanes = kt_ref.shape[1]
    for j in range(tiles):
        half[j] = jnp.broadcast_to(0.5 * kt_ref[j // lanes, j % lanes : j % lanes + 1, :], (8, 128))

    def block(b, carry):
        def at(h):
            return pl.ds(pl.multiple_of(b * BLOCK + 8 * h, 8), 8)

        mine = [ks_ref[at(h), :] for h in range(BLOCK // 8)]

        def tile(q, carry):
            lanes = pl.ds(pl.multiple_of(q * 128, 128), 128)
            other = half[q]
            for h in range(BLOCK // 8):
                v = s_ref[at(h), lanes]
                held[at(h), lanes] = jnp.where(v == excluded_score, jnp.float32(0.0), v / (mine[h] + other))
            return carry

        lax.fori_loop(0, tiles, tile, 0, unroll=4)
        span = pl.ds(pl.multiple_of(b * BLOCK, BLOCK), BLOCK)
        pltpu.make_async_copy(held.at[span], out_ref.at[span], sem.at[0]).start()
        return carry

    lax.fori_loop(0, rows // BLOCK, block, 0)
    pltpu.make_async_copy(held, out_ref, sem.at[0]).wait()


def body(ns, nt, src_emb, tgt_emb, src_ids, tgt_ids):
    rows, part = src_emb.shape
    cols, feats = tgt_emb.shape
    width = part * nt
    nz = ns // 4
    cw = min(CHUNK, cols)
    chunks = cols // cw
    lanes = cw // 128
    f32, bf16 = jnp.float32, jnp.bfloat16
    dma = pltpu.SemaphoreType.DMA
    hbm = pl.BlockSpec(memory_space=pltpu.MemorySpace.HBM)
    vmem = pl.BlockSpec(memory_space=pltpu.VMEM)
    args = (tgt_emb.T, src_emb, src_ids.reshape(1, rows), tgt_ids.reshape(1, cols))
    scores, kt, ks = pl.pallas_call(
        functools.partial(kernel, (ns, nt, nz, chunks, cw, feats)),
        out_shape=(
            jax.ShapeDtypeStruct((rows, cols), f32),
            jax.ShapeDtypeStruct((chunks, lanes, 128), f32),
            jax.ShapeDtypeStruct((rows, 128), f32),
        ),
        in_specs=[hbm, hbm, hbm, hbm],
        out_specs=(vmem, vmem, vmem),
        scratch_shapes=[
            pltpu.VMEM((1, rows), jnp.int32),
            pltpu.VMEM((1, cols), jnp.int32),
            pltpu.VMEM((rows, 128), jnp.int32),
            pltpu.VMEM((chunks, nz, 2, 2, feats, cw), bf16),
            pltpu.VMEM((rows, width), bf16),
            pltpu.VMEM((rows, width), bf16),
            pltpu.VMEM((4, rows, 128), f32),
            pltpu.VMEM((chunks, 4 * lanes, 128), bf16),
            pltpu.VMEM((ns, 4 * lanes, 128), bf16),
            pltpu.VMEM((ns, 4 * lanes, 128), bf16),
            pltpu.VMEM((lanes, 128), f32),
            pltpu.VMEM((8, rows), f32),
            pltpu.VMEM((nt, 8, rows), f32),
            dma((chunks, nz)),
            dma((2, 2, nz)),
            dma((chunks,)),
            dma((2,)),
            dma((chunks,)),
            dma((1,)),
            dma((nt,)),
            dma((1,)),
            dma((1,)),
            dma((1,)),
            dma((1,)),
            dma((1,)),
            dma((1,)),
            dma((1,)),
            dma((1,)),
            dma((1,)),
            dma((4,)),
        ],
        compiler_params=pltpu.CompilerParams(
            collective_id=0, has_side_effects=True, vmem_limit_bytes=40 * 2**20
        ),
    )(*(pltpu.with_memory_space_constraint(v, pltpu.MemorySpace.HBM) for v in args))
    return pl.pallas_call(
        finish,
        out_shape=jax.ShapeDtypeStruct((rows, cols), f32),
        in_specs=[vmem, vmem, vmem],
        out_specs=pl.BlockSpec(memory_space=pl.ANY),
        scratch_shapes=[
            pltpu.VMEM((cols // 128, 8, 128), f32),
            pltpu.VMEM((rows, cols), f32),
            dma((1,)),
        ],
        compiler_params=pltpu.CompilerParams(vmem_limit_bytes=40 * 2**20),
    )(scores, kt, ks)


def solution(mesh):
    return jax.shard_map(
        functools.partial(body, mesh.shape["src"], mesh.shape["tgt"]),
        mesh=mesh,
        in_specs=(P("src", "tgt"), P("tgt", "src"), P("src"), P("tgt")),
        out_specs=P("src", "tgt"),
        check_vma=False,
    )
```

```python
import functools

import jax
import jax.numpy as jnp
from jax import lax
from jax.experimental import pallas as pl
from jax.experimental.pallas import tpu as pltpu
from jax.sharding import PartitionSpec as P

epsilon = 1e-06
excluded_score = -2.0
MESH = pl.DeviceIdType.MESH
CHUNK = 512
FIRST_LEAD = 1
FIRST_GAP = 1
Z_AHEAD = 3
Y_AHEAD = 7
BLOCK = 32
HOP = 1
Y_LAG = 2
CORE_LAG = 1
NORM_AT = -1


def sort4(v):
    a, b = jnp.maximum(v[0], v[1]), jnp.minimum(v[0], v[1])
    c, d = jnp.maximum(v[2], v[3]), jnp.minimum(v[2], v[3])
    top, e = jnp.maximum(a, c), jnp.minimum(a, c)
    f, low = jnp.maximum(b, d), jnp.minimum(b, d)
    return (top, jnp.maximum(e, f), jnp.minimum(e, f), low)


def merge(first, second):
    c = [jnp.maximum(first[k], second[3 - k]) for k in range(4)]
    a, b = jnp.maximum(c[0], c[2]), jnp.maximum(c[1], c[3])
    d, e = jnp.minimum(c[0], c[2]), jnp.minimum(c[1], c[3])
    return (jnp.maximum(a, b), jnp.minimum(a, b), jnp.maximum(d, e), jnp.minimum(d, e))


def insert(best, value):
    out = []
    for level in best[:-1]:
        out.append(jnp.maximum(level, value))
        value = jnp.minimum(level, value)
    out.append(jnp.maximum(best[-1], value))
    return tuple(out)


def absorb(best, values):
    whole = len(values) // 4 * 4
    for k in range(0, whole, 4):
        best = merge(best, sort4(values[k : k + 4]))
    for value in values[whole:]:
        best = insert(best, value)
    return best


def fold_sublanes(best, shifts=(4, 2, 1)):
    for shift in shifts:
        best = merge(best, tuple(pltpu.roll(level, shift, 0) for level in best))
    return best


def mean_of(best):
    return (best[0] + best[1] + best[2] + best[3]) * 0.25


def lowest(shape):
    return tuple(jnp.full(shape, -jnp.inf, jnp.float32) for _ in range(4))


def kernel(dims, x_ref, a_ref, sid_ref, tid_ref, s_out, kt_out, ks_out, sid, tid, sids, g, a_whole, a_unit, raw, rowbest,
           colbuf, colin, tailin, ktown, rowbuf, rowin, zrecv, zsend, yrecv, ysend, crecv, csend, arecv, asend, rrecv,
           rsend, krecv, ksend, mrecv, msend, trecv, tsend, lsem):
    ns, nt, nz, chunks, cw, feats = dims
    s = lax.axis_index("src")
    t = lax.axis_index("tgt")
    z, y, c = s // 4, (s // 2) % 2, s % 2
    right = (s + 4, t)
    left = (s - 4, t)
    over = (z * 4 + (1 - y) * 2 + c, t)
    core = (s + 1 - 2 * c, t)
    rows, width = a_unit.shape
    part = a_ref.shape[1]
    lanes = cw // 128
    first = chunks - 1
    last = first - 1
    stride = ns // chunks
    has_right, has_left = z + 1 < nz, z >= 1

    def remote(src, dst, send, recv, where):
        return pltpu.make_async_remote_copy(
            src_ref=src, dst_ref=dst, send_sem=send, recv_sem=recv, device_id=where, device_id_type=MESH
        )

    def chunk_cols(j):
        return pl.ds(pl.multiple_of(j * cw, cw), cw)

    barrier = pltpu.get_barrier_semaphore()

    @pl.when(has_right)
    def _():
        pl.semaphore_signal(barrier, inc=1, device_id=right, device_id_type=MESH)

    @pl.when(has_left)
    def _():
        pl.semaphore_signal(barrier, inc=1, device_id=left, device_id_type=MESH)

    pl.semaphore_signal(barrier, inc=1, device_id=over, device_id_type=MESH)
    pl.semaphore_signal(barrier, inc=1, device_id=core, device_id_type=MESH)
    for k in range(1, nt):
        pl.semaphore_signal(barrier, inc=1, device_id=(s, lax.rem(t + k, nt)), device_id_type=MESH)

    for j in range(chunks):
        pltpu.make_async_copy(x_ref.at[:, chunk_cols(j)], g.at[j, z, y, c], lsem.at[0]).start()
    acols = pl.ds(pl.multiple_of(t * part, part), part)
    local_a = pltpu.make_async_copy(a_ref, a_whole.at[:, acols], lsem.at[1])
    local_sid = pltpu.make_async_copy(sid_ref, sid, lsem.at[2])
    local_tid = pltpu.make_async_copy(tid_ref, tid, lsem.at[3])
    local_a.start()
    local_sid.start()
    local_tid.start()
    pl.semaphore_wait(barrier, 1 + nt + has_right.astype(jnp.int32) + has_left.astype(jnp.int32))

    def to_right(j, zp, own=False):
        ref = g.at[j, zp, y, c]
        return remote(x_ref.at[:, chunk_cols(j)] if own else ref, ref, zsend.at[0, 0, zp], zrecv.at[j, zp], right)

    def to_left(j, zp, own=False):
        ref = g.at[j, zp, y, c]
        return remote(x_ref.at[:, chunk_cols(j)] if own else ref, ref, zsend.at[1, 0, zp], zrecv.at[j, zp], left)

    def both_right(zp):
        ref = g.at[first, zp, :, c]
        return remote(ref, ref, zsend.at[0, 1, zp], zrecv.at[first, zp], right)

    def both_left(zp):
        ref = g.at[first, zp, :, c]
        return remote(ref, ref, zsend.at[1, 1, zp], zrecv.at[first, zp], left)

    far = jnp.where(z < nz // 2, nz - 1, 0)
    near = pl.ds(jnp.where(z < nz // 2, 0, 1), nz - 1)

    def to_over(j, zp, own=False):
        ref = g.at[j, zp, y, c]
        src = x_ref.at[:, chunk_cols(j)] if own else ref
        slot = jnp.where(jnp.logical_and(j == last, zp == far), chunks, j)
        return remote(src, ref, ysend.at[0], yrecv.at[slot], over)

    def from_over(j):
        ref = g.at[j, :, 1 - y, c]
        return remote(ref, ref, ysend.at[0], yrecv.at[j], over)

    def swap(own):
        ref = g.at[first, z, y, c] if own else g.at[first, z, 1 - y, c]
        return remote(x_ref.at[:, chunk_cols(first)] if own else ref, ref, ysend.at[1], yrecv.at[first], over)

    def to_core(j, yy):
        ref = g.at[j, :, yy, c]
        return remote(ref, ref, csend.at[0], crecv.at[j], core)

    def from_core(j):
        ref = g.at[j, :, :, 1 - c]
        return remote(ref, ref, csend.at[0], crecv.at[j], core)

    def to_tgt(k):
        return remote(a_ref, a_whole.at[:, acols], asend.at[0], arecv.at[t], (s, lax.rem(t + k, nt)))

    z_ahead, y_ahead = min(Z_AHEAD, first - 1), min(Y_AHEAD, first)
    depth = HOP * (nz - 1)
    sides = ((to_left, has_left, HOP * z - depth), (to_right, has_right, -HOP * z))
    swap(True).start()
    for j in range(max(y_ahead, z_ahead)):
        if j < y_ahead:
            to_over(j, z, True).start()
        if j < z_ahead:
            for to_side, there, lead in sides:

                @pl.when(jnp.logical_and(there, j < lead + z_ahead))
                def _():
                    to_side(j, z, True).start()

    for k in range(1, nt):
        to_tgt(k).start()
    pltpu.make_async_copy(g.at[:, z, y, c], g.at[:, z, y, c], lsem.at[0]).wait()
    swap(False).wait_recv()
    local_sid.wait()
    local_tid.wait()
    sids[...] = jnp.broadcast_to(sid[...], (128, rows)).T
    for k in range(4):
        rowbest[k] = jnp.full(rowbest.shape[1:], -jnp.inf, jnp.float32)

    def normalize_sources():
        local_a.wait()
        for k in range(1, nt):
            other = lax.rem(t + k, nt)
            cols = pl.ds(pl.multiple_of(other * part, part), part)
            remote(a_ref, a_whole.at[:, cols], asend.at[0], arecv.at[other], (s, other)).wait_recv()
        block = 16

        def step(r, carry):
            at = pl.ds(pl.multiple_of(r * block, block), block)
            v = a_whole[at, :].astype(jnp.float32)
            scale = jnp.sqrt(jnp.sum(v * v, axis=1, keepdims=True) + epsilon)
            a_unit[at, :] = (v / scale).astype(jnp.bfloat16)
            return carry

        lax.fori_loop(0, rows // block, step, 0, unroll=2)

    def compute(j):
        cols = chunk_cols(j)
        found = g[j].reshape(width, cw)
        raw[...] = jnp.dot(a_unit[...], found, preferred_element_type=jnp.float32)
        found = found.astype(jnp.float32)
        acc = jnp.sum((found * found).reshape(width // 8, 8, cw), axis=0)
        inverse = jnp.broadcast_to(1.0 / jnp.sqrt(jnp.sum(acc, axis=0, keepdims=True) + epsilon), (8, cw))
        tids = jnp.broadcast_to(tid[:, cols], (8, cw))

        def group(r, best):
            ats = [pl.ds(pl.multiple_of(r * 32 + h * 8, 8), 8) for h in range(4)]
            spans = [slice(q * 128, (q + 1) * 128) for q in range(lanes)]
            ids = [sids[at, :] for at in ats]
            found = [[raw[at, span] for span in spans] for at in ats]
            rows_in = [tuple(rowbest[k, at, :] for k in range(4)) for at in ats]
            found = [
                [jnp.where(ids[h] == tids[:, span], jnp.float32(excluded_score), v * inverse[:, span]) for v, span in zip(found[h], spans)]
                for h in range(4)
            ]
            rows_out = [absorb(rows_in[h], found[h]) for h in range(4)]
            best = tuple(absorb(best[q], [found[h][q] for h in range(4)]) for q in range(lanes))
            for h, at in enumerate(ats):
                for q in range(lanes):
                    s_out[at, pl.ds(pl.multiple_of(j * cw + q * 128, 128), 128)] = found[h][q]
                for k in range(4):
                    rowbest[k, at, :] = rows_out[h][k]
            return best

        best = lax.fori_loop(0, rows // 32, group, tuple(lowest((8, 128)) for _ in range(lanes)), unroll=1)
        best = [fold_sublanes(b) for b in best]
        row = lax.broadcasted_iota(jnp.int32, (8, 128), 0)
        tiles = []
        for q in range(0, lanes, 2):
            out = best[q][0]
            for k in range(1, 8):
                out = jnp.where(row == k, best[q + k // 4][k % 4], out)
            tiles.append(out)
        colbuf[j] = jnp.concatenate(tiles, axis=0).astype(jnp.bfloat16)

    def send_columns(j):
        owner = j * stride

        @pl.when(s != owner)
        def _():
            remote(colbuf.at[j], colin.at[s], ksend.at[0], krecv.at[0], (owner, t)).start()

        @pl.when(s == owner)
        def _():
            colin[s] = colbuf[j]

    def knn_of(ref):
        best = absorb(lowest((4 * lanes, 128)), [ref[p].astype(jnp.float32) for p in range(ns)])
        mean = mean_of(fold_sublanes(best, (2, 1)))
        return jnp.concatenate([mean[4 * q + 3 : 4 * q + 4] for q in range(lanes)], axis=0)

    def mean_copy(k):
        j = s // stride
        return remote(ktown, kt_out.at[j], msend.at[0], mrecv.at[0], (lax.rem(s + k, ns), t))

    def merge_columns(j):
        @pl.when(s == j * stride)
        def _():
            ref = colin.at[pl.ds(0, ns - 1)]
            remote(ref, ref, ksend.at[0], krecv.at[0], core).wait_recv()
            ktown[...] = knn_of(colin)
            for k in range(1, ns):
                mean_copy(k).start()
            kt_out[j] = ktown[...]

    def within(j):
        return jnp.logical_and(j >= 0, j < first)

    def relay(to_side, there, behind_me, j):
        for d in range(1, nz):
            zp, present = behind_me(d)

            @pl.when(present)
            def _():
                to_side(j, zp).wait_recv()

                @pl.when(there)
                def _():
                    to_side(j, zp).start()

                to_over(j, zp).start()

    relays = (
        functools.partial(relay, to_left, has_left, lambda d: (z + d, z + d < nz)),
        functools.partial(relay, to_right, has_right, lambda d: (z - d, z - d >= 0)),
    )

    sides_both = (
        (both_left, has_left, HOP * z - depth, lambda d: (z + d, z + d < nz)),
        (both_right, has_right, -HOP * z, lambda d: (z - d, z - d >= 0)),
    )

    y_behind = depth + Y_LAG
    behind = y_behind + CORE_LAG

    def for_peers(what):
        for q in range(nz):
            zz = jnp.where(z < nz // 2, nz - 1 - q, q)
            for a in (1, 0):
                for b in (1, 0):
                    to = zz * 4 + lax.rem(y + a, 2) * 2 + lax.rem(c + b, 2)
                    if a or b:
                        what(to)
                    else:
                        pl.when(zz != z)(functools.partial(what, to))

    def tail_copy(e, to):
        src = colbuf.at[first - e]
        return remote(src, tailin.at[e, s], tsend.at[0], trecv.at[e], (to, t))

    def y_done(j):
        from_over(j).wait_recv()
        to_core(j, 1 - y).start()

    def tick(i, carry):
        for (to_side, there, lead), relay_side in zip(sides, relays):
            j = i + lead

            @pl.when(jnp.logical_and(within(j + z_ahead), there))
            def _():
                to_side(j + z_ahead, z, True).start()

            @pl.when(within(j))
            def _():
                relay_side(j)

        j = i - depth

        @pl.when(jnp.logical_and(j >= 0, j + y_ahead < first))
        def _():
            to_over(j + y_ahead, z, True).start()

        @pl.when(within(j))
        def _():
            to_core(j, y).start()

        m = i - behind
        jc = jnp.where(m == last, first, jnp.where(m == first, last, m))

        @pl.when(m == NORM_AT)
        def _():
            normalize_sources()

        @pl.when(m == last)
        def _():
            for which, slot in ((near, last), (pl.ds(far, 1), chunks)):
                ref = g.at[last, which, 1 - y, c]
                remote(ref, ref, ysend.at[0], yrecv.at[slot], over).wait_recv()
                ref = g.at[last, which, 1 - y, c]
                remote(ref, ref, csend.at[0], crecv.at[last], core).start()
            for j in range(last):
                merge_columns(j)

        @pl.when(m >= 0)
        def _():
            from_core(jc).wait_recv()
            compute(jc)


        @pl.when(jnp.logical_and(m >= 0, m < last))
        def _():
            send_columns(jc)

        @pl.when(m >= last)
        def _():
            for_peers(lambda to: tail_copy(m - last, to).start())
            tailin[m - last, s] = colbuf[jc]

        for both, there, lead, behind_me in sides_both:

            @pl.when(jnp.logical_and(i == first - lead - FIRST_LEAD, there))
            def _():
                both(z).start()

        final = last - 1 + behind
        for d in range(1, nz):
            for both, there, lead, behind_me in sides_both:
                zp, present = behind_me(d)
                at = jnp.where(there, jnp.minimum(first - lead + FIRST_GAP * (d - 1), final), final)

                @pl.when(jnp.logical_and(present, i == at))
                def _():
                    both(zp).wait_recv()

                    @pl.when(there)
                    def _():
                        both(zp).start()

        @pl.when(i == final)
        def _():
            to_core(first, y).start()
            to_core(first, 1 - y).start()

        jy = i - y_behind

        @pl.when(jnp.logical_and(jy >= 0, jy < last))
        def _():
            y_done(jy)

        return carry

    lax.fori_loop(0, chunks + behind, tick, 0)

    def row_copy(k):
        return remote(rowbuf, rowin.at[t], rsend.at[0], rrecv.at[0], (s, lax.rem(t + k, nt)))

    flat = [rowbest[k].T for k in range(4)]
    best = lowest((8, rows))
    for q in range(128 // 8):
        best = merge(best, tuple(flat[k][q * 8 : (q + 1) * 8, :] for k in range(4)))
    best = fold_sublanes(best)
    row = lax.broadcasted_iota(jnp.int32, (8, rows), 0)
    out = jnp.full((8, rows), -jnp.inf, jnp.float32)
    for k in range(4):
        out = jnp.where(row == k, best[k], out)
    rowbuf[...] = out
    rowin[t] = out
    for k in range(1, nt):
        row_copy(k).start()

    def drain_z(zp, kind, ref):
        @pl.when(jnp.logical_and(has_right, zp <= z))
        def _():
            remote(ref, ref, zsend.at[0, kind, zp], zrecv.at[0, zp], right).wait_send()

        @pl.when(jnp.logical_and(has_left, zp >= z))
        def _():
            remote(ref, ref, zsend.at[1, kind, zp], zrecv.at[0, zp], left).wait_send()

    for zp in range(nz):
        drain_z(zp, 0, g.at[pl.ds(0, first), 0, 0, 0])
        drain_z(zp, 1, g.at[0, 0, :, 0])
    ref = g.at[pl.ds(0, first), :, 0, 0]
    remote(ref, ref, ysend.at[0], yrecv.at[0], over).wait_send()
    swap(True).wait_send()
    ref = g.at[:, :, :, c]
    remote(ref, ref, csend.at[0], crecv.at[0], core).wait_send()
    for k in range(1, nt):
        to_tgt(k).wait_send()

    for e in range(2):
        ref = tailin.at[e, pl.ds(0, ns - 1)]
        remote(ref, ref, tsend.at[0], trecv.at[e], core).wait_recv()
        kt_out[first - e] = knn_of(tailin.at[e])
    for k in range(1, nt):
        row_copy(k).wait_send()
    ref = rowin.at[pl.ds(0, nt - 1)]
    remote(ref, ref, rsend.at[0], rrecv.at[0], core).wait_recv()
    half = 0.5 * mean_of(fold_sublanes(absorb(lowest((8, rows)), [rowin[p] for p in range(nt)])))
    ks_out[...] = jnp.broadcast_to(half[0:1], (128, rows)).T

    owns = jnp.logical_and(lax.rem(s, stride) == 0, s < last * stride)

    @pl.when(owns)
    def _():
        ref = colbuf.at[pl.ds(0, last - 1)]
        remote(ref, ref, ksend.at[0], krecv.at[0], core).wait_send()
        mean = kt_out.at[pl.ds(0, last - 1)]
        remote(mean, mean, msend.at[0], mrecv.at[0], core).wait_recv()
        for k in range(1, ns):
            mean_copy(k).wait_send()

    @pl.when(jnp.logical_not(owns))
    def _():
        ref = colbuf.at[pl.ds(0, last)]
        remote(ref, ref, ksend.at[0], krecv.at[0], core).wait_send()
        mean = kt_out.at[pl.ds(0, last)]
        remote(mean, mean, msend.at[0], mrecv.at[0], core).wait_recv()

    ref = tailin.at[:, pl.ds(0, ns - 1)]
    remote(ref, ref, tsend.at[0], trecv.at[0], core).wait_send()


def finish(s_ref, kt_ref, ks_ref, out_ref, half, held, sem):
    rows, cols = s_ref.shape
    tiles = cols // 128
    lanes = kt_ref.shape[1]
    for j in range(tiles):
        half[j] = jnp.broadcast_to(0.5 * kt_ref[j // lanes, j % lanes : j % lanes + 1, :], (8, 128))

    def block(b, carry):
        def at(h):
            return pl.ds(pl.multiple_of(b * BLOCK + 8 * h, 8), 8)

        mine = [ks_ref[at(h), :] for h in range(BLOCK // 8)]

        def tile(q, carry):
            lanes = pl.ds(pl.multiple_of(q * 128, 128), 128)
            other = half[q]
            for h in range(BLOCK // 8):
                v = s_ref[at(h), lanes]
                held[at(h), lanes] = jnp.where(v == excluded_score, jnp.float32(0.0), v / (mine[h] + other))
            return carry

        lax.fori_loop(0, tiles, tile, 0, unroll=4)
        span = pl.ds(pl.multiple_of(b * BLOCK, BLOCK), BLOCK)
        pltpu.make_async_copy(held.at[span], out_ref.at[span], sem.at[0]).start()
        return carry

    lax.fori_loop(0, rows // BLOCK, block, 0)
    pltpu.make_async_copy(held, out_ref, sem.at[0]).wait()


def body(ns, nt, src_emb, tgt_emb, src_ids, tgt_ids):
    rows, part = src_emb.shape
    cols, feats = tgt_emb.shape
    width = part * nt
    nz = ns // 4
    cw = min(CHUNK, cols)
    chunks = cols // cw
    lanes = cw // 128
    f32, bf16 = jnp.float32, jnp.bfloat16
    dma = pltpu.SemaphoreType.DMA
    hbm = pl.BlockSpec(memory_space=pltpu.MemorySpace.HBM)
    vmem = pl.BlockSpec(memory_space=pltpu.VMEM)
    args = (tgt_emb.T, src_emb, src_ids.reshape(1, rows), tgt_ids.reshape(1, cols))
    scores, kt, ks = pl.pallas_call(
        functools.partial(kernel, (ns, nt, nz, chunks, cw, feats)),
        out_shape=(
            jax.ShapeDtypeStruct((rows, cols), f32),
            jax.ShapeDtypeStruct((chunks, lanes, 128), f32),
            jax.ShapeDtypeStruct((rows, 128), f32),
        ),
        in_specs=[hbm, hbm, hbm, hbm],
        out_specs=(vmem, vmem, vmem),
        scratch_shapes=[
            pltpu.VMEM((1, rows), jnp.int32),
            pltpu.VMEM((1, cols), jnp.int32),
            pltpu.VMEM((rows, 128), jnp.int32),
            pltpu.VMEM((chunks, nz, 2, 2, feats, cw), bf16),
            pltpu.VMEM((rows, width), bf16),
            pltpu.VMEM((rows, width), bf16),
            pltpu.VMEM((rows, cw), f32),
            pltpu.VMEM((4, rows, 128), f32),
            pltpu.VMEM((chunks, 4 * lanes, 128), bf16),
            pltpu.VMEM((ns, 4 * lanes, 128), bf16),
            pltpu.VMEM((2, ns, 4 * lanes, 128), bf16),
            pltpu.VMEM((lanes, 128), f32),
            pltpu.VMEM((8, rows), f32),
            pltpu.VMEM((nt, 8, rows), f32),
            dma((chunks, nz)),
            dma((2, 2, nz)),
            dma((chunks + 1,)),
            dma((2,)),
            dma((chunks,)),
            dma((1,)),
            dma((nt,)),
            dma((1,)),
            dma((1,)),
            dma((1,)),
            dma((1,)),
            dma((1,)),
            dma((1,)),
            dma((1,)),
            dma((2,)),
            dma((1,)),
            dma((4,)),
        ],
        compiler_params=pltpu.CompilerParams(
            collective_id=0, has_side_effects=True, vmem_limit_bytes=40 * 2**20
        ),
    )(*(pltpu.with_memory_space_constraint(v, pltpu.MemorySpace.HBM) for v in args))
    return pl.pallas_call(
        finish,
        out_shape=jax.ShapeDtypeStruct((rows, cols), f32),
        in_specs=[vmem, vmem, vmem],
        out_specs=pl.BlockSpec(memory_space=pl.ANY),
        scratch_shapes=[
            pltpu.VMEM((cols // 128, 8, 128), f32),
            pltpu.VMEM((rows, cols), f32),
            dma((1,)),
        ],
        compiler_params=pltpu.CompilerParams(vmem_limit_bytes=40 * 2**20),
    )(scores, kt, ks)


def solution(mesh):
    return jax.shard_map(
        functools.partial(body, mesh.shape["src"], mesh.shape["tgt"]),
        mesh=mesh,
        in_specs=(P("src", "tgt"), P("tgt", "src"), P("src"), P("tgt")),
        out_specs=P("src", "tgt"),
        check_vma=False,
    )
```

```python
import functools

import jax
import jax.numpy as jnp
from jax import lax
from jax.experimental import pallas as pl
from jax.experimental.pallas import tpu as pltpu
from jax.sharding import PartitionSpec as P

epsilon = 1e-06
excluded_score = -2.0
MESH = pl.DeviceIdType.MESH
CHUNK = 512
FIRST_LEAD = 1
FIRST_GAP = 1
Z_AHEAD = 3
Y_AHEAD = 7
BLOCK = 32
HOP = 1
Y_LAG = 2
CORE_LAG = 1
NORM_AT = -1


def sort4(v):
    a, b = jnp.maximum(v[0], v[1]), jnp.minimum(v[0], v[1])
    c, d = jnp.maximum(v[2], v[3]), jnp.minimum(v[2], v[3])
    top, e = jnp.maximum(a, c), jnp.minimum(a, c)
    f, low = jnp.maximum(b, d), jnp.minimum(b, d)
    return (top, jnp.maximum(e, f), jnp.minimum(e, f), low)


def merge(first, second):
    c = [jnp.maximum(first[k], second[3 - k]) for k in range(4)]
    a, b = jnp.maximum(c[0], c[2]), jnp.maximum(c[1], c[3])
    d, e = jnp.minimum(c[0], c[2]), jnp.minimum(c[1], c[3])
    return (jnp.maximum(a, b), jnp.minimum(a, b), jnp.maximum(d, e), jnp.minimum(d, e))


def insert(best, value):
    out = []
    for level in best[:-1]:
        out.append(jnp.maximum(level, value))
        value = jnp.minimum(level, value)
    out.append(jnp.maximum(best[-1], value))
    return tuple(out)


def absorb(best, values):
    whole = len(values) // 4 * 4
    for k in range(0, whole, 4):
        best = merge(best, sort4(values[k : k + 4]))
    for value in values[whole:]:
        best = insert(best, value)
    return best


def fold_sublanes(best, shifts=(4, 2, 1)):
    for shift in shifts:
        best = merge(best, tuple(pltpu.roll(level, shift, 0) for level in best))
    return best


def mean_of(best):
    return (best[0] + best[1] + best[2] + best[3]) * 0.25


def lowest(shape):
    return tuple(jnp.full(shape, -jnp.inf, jnp.float32) for _ in range(4))


def kernel(dims, x_ref, a_ref, sid_ref, tid_ref, s_out, kt_out, ks_out, sid, tid, sids, g, a_whole, a_unit, raw, rowbest,
           colbuf, colin, tailin, ktown, rowbuf, rowin, zrecv, zsend, yrecv, ysend, crecv, csend, arecv, asend, rrecv,
           rsend, krecv, ksend, mrecv, msend, trecv, tsend, lsem):
    ns, nt, nz, chunks, cw, feats = dims
    s = lax.axis_index("src")
    t = lax.axis_index("tgt")
    z, y, c = s // 4, (s // 2) % 2, s % 2
    right = (s + 4, t)
    left = (s - 4, t)
    over = (z * 4 + (1 - y) * 2 + c, t)
    core = (s + 1 - 2 * c, t)
    rows, width = a_unit.shape
    part = a_ref.shape[1]
    lanes = cw // 128
    first = chunks - 1
    last = first - 1
    stride = ns // chunks
    has_right, has_left = z + 1 < nz, z >= 1

    def remote(src, dst, send, recv, where):
        return pltpu.make_async_remote_copy(
            src_ref=src, dst_ref=dst, send_sem=send, recv_sem=recv, device_id=where, device_id_type=MESH
        )

    def chunk_cols(j):
        return pl.ds(pl.multiple_of(j * cw, cw), cw)

    barrier = pltpu.get_barrier_semaphore()

    @pl.when(has_right)
    def _():
        pl.semaphore_signal(barrier, inc=1, device_id=right, device_id_type=MESH)

    @pl.when(has_left)
    def _():
        pl.semaphore_signal(barrier, inc=1, device_id=left, device_id_type=MESH)

    pl.semaphore_signal(barrier, inc=1, device_id=over, device_id_type=MESH)
    pl.semaphore_signal(barrier, inc=1, device_id=core, device_id_type=MESH)
    for k in range(1, nt):
        pl.semaphore_signal(barrier, inc=1, device_id=(s, lax.rem(t + k, nt)), device_id_type=MESH)

    for j in range(chunks):
        pltpu.make_async_copy(x_ref.at[:, chunk_cols(j)], g.at[j, z, y, c], lsem.at[0]).start()
    acols = pl.ds(pl.multiple_of(t * part, part), part)
    local_a = pltpu.make_async_copy(a_ref, a_whole.at[:, acols], lsem.at[1])
    local_sid = pltpu.make_async_copy(sid_ref, sid, lsem.at[2])
    local_tid = pltpu.make_async_copy(tid_ref, tid, lsem.at[3])
    local_a.start()
    local_sid.start()
    local_tid.start()
    pl.semaphore_wait(barrier, 1 + nt + has_right.astype(jnp.int32) + has_left.astype(jnp.int32))

    def to_right(j, zp, own=False):
        ref = g.at[j, zp, y, c]
        return remote(x_ref.at[:, chunk_cols(j)] if own else ref, ref, zsend.at[0, 0, zp], zrecv.at[j, zp], right)

    def to_left(j, zp, own=False):
        ref = g.at[j, zp, y, c]
        return remote(x_ref.at[:, chunk_cols(j)] if own else ref, ref, zsend.at[1, 0, zp], zrecv.at[j, zp], left)

    def both_right(zp):
        ref = g.at[first, zp, :, c]
        return remote(ref, ref, zsend.at[0, 1, zp], zrecv.at[first, zp], right)

    def both_left(zp):
        ref = g.at[first, zp, :, c]
        return remote(ref, ref, zsend.at[1, 1, zp], zrecv.at[first, zp], left)

    far = jnp.where(z < nz // 2, nz - 1, 0)
    near = pl.ds(jnp.where(z < nz // 2, 0, 1), nz - 1)

    def to_over(j, zp, own=False):
        ref = g.at[j, zp, y, c]
        src = x_ref.at[:, chunk_cols(j)] if own else ref
        slot = jnp.where(jnp.logical_and(j == last, zp == far), chunks, j)
        return remote(src, ref, ysend.at[0], yrecv.at[slot], over)

    def from_over(j):
        ref = g.at[j, :, 1 - y, c]
        return remote(ref, ref, ysend.at[0], yrecv.at[j], over)

    def swap(own):
        ref = g.at[first, z, y, c] if own else g.at[first, z, 1 - y, c]
        return remote(x_ref.at[:, chunk_cols(first)] if own else ref, ref, ysend.at[1], yrecv.at[first], over)

    def to_core(j, yy):
        ref = g.at[j, :, yy, c]
        return remote(ref, ref, csend.at[0], crecv.at[j], core)

    def from_core(j):
        ref = g.at[j, :, :, 1 - c]
        return remote(ref, ref, csend.at[0], crecv.at[j], core)

    def to_tgt(k):
        return remote(a_ref, a_whole.at[:, acols], asend.at[0], arecv.at[t], (s, lax.rem(t + k, nt)))

    z_ahead, y_ahead = min(Z_AHEAD, first - 1), min(Y_AHEAD, first)
    depth = HOP * (nz - 1)
    sides = ((to_left, has_left, HOP * z - depth), (to_right, has_right, -HOP * z))
    swap(True).start()
    for j in range(max(y_ahead, z_ahead)):
        if j < y_ahead:
            to_over(j, z, True).start()
        if j < z_ahead:
            for to_side, there, lead in sides:

                @pl.when(jnp.logical_and(there, j < lead + z_ahead))
                def _():
                    to_side(j, z, True).start()

    for k in range(1, nt):
        to_tgt(k).start()
    pltpu.make_async_copy(g.at[:, z, y, c], g.at[:, z, y, c], lsem.at[0]).wait()
    swap(False).wait_recv()
    local_sid.wait()
    local_tid.wait()
    sids[...] = jnp.broadcast_to(sid[...], (128, rows)).T
    for k in range(4):
        rowbest[k] = jnp.full(rowbest.shape[1:], -jnp.inf, jnp.float32)

    def normalize_sources():
        local_a.wait()
        for k in range(1, nt):
            other = lax.rem(t + k, nt)
            cols = pl.ds(pl.multiple_of(other * part, part), part)
            remote(a_ref, a_whole.at[:, cols], asend.at[0], arecv.at[other], (s, other)).wait_recv()
        block = 16

        def step(r, carry):
            at = pl.ds(pl.multiple_of(r * block, block), block)
            v = a_whole[at, :].astype(jnp.float32)
            scale = jnp.sqrt(jnp.sum(v * v, axis=1, keepdims=True) + epsilon)
            a_unit[at, :] = (v / scale).astype(jnp.bfloat16)
            return carry

        lax.fori_loop(0, rows // block, step, 0, unroll=2)

    def compute(j):
        cols = chunk_cols(j)
        found = g[j].reshape(width, cw)
        raw[...] = jnp.dot(a_unit[...], found, preferred_element_type=jnp.float32)
        found = found.astype(jnp.float32)
        acc = jnp.sum((found * found).reshape(width // 8, 8, cw), axis=0)
        inverse = jnp.broadcast_to(1.0 / jnp.sqrt(jnp.sum(acc, axis=0, keepdims=True) + epsilon), (8, cw))
        tids = jnp.broadcast_to(tid[:, cols], (8, cw))

        def group(r, best):
            ats = [pl.ds(pl.multiple_of(r * 32 + h * 8, 8), 8) for h in range(4)]
            spans = [slice(q * 128, (q + 1) * 128) for q in range(lanes)]
            ids = [sids[at, :] for at in ats]
            found = [[raw[at, span] for span in spans] for at in ats]
            rows_in = [tuple(rowbest[k, at, :] for k in range(4)) for at in ats]
            found = [
                [jnp.where(ids[h] == tids[:, span], jnp.float32(excluded_score), v * inverse[:, span]) for v, span in zip(found[h], spans)]
                for h in range(4)
            ]
            rows_out = [absorb(rows_in[h], found[h]) for h in range(4)]
            best = tuple(absorb(best[q], [found[h][q] for h in range(4)]) for q in range(lanes))
            for h, at in enumerate(ats):
                for q in range(lanes):
                    s_out[at, pl.ds(pl.multiple_of(j * cw + q * 128, 128), 128)] = found[h][q]
                for k in range(4):
                    rowbest[k, at, :] = rows_out[h][k]
            return best

        best = lax.fori_loop(0, rows // 32, group, tuple(lowest((8, 128)) for _ in range(lanes)), unroll=1)
        best = [fold_sublanes(b) for b in best]
        row = lax.broadcasted_iota(jnp.int32, (8, 128), 0)
        tiles = []
        for q in range(0, lanes, 2):
            out = best[q][0]
            for k in range(1, 8):
                out = jnp.where(row == k, best[q + k // 4][k % 4], out)
            tiles.append(out)
        colbuf[j] = jnp.concatenate(tiles, axis=0).astype(jnp.bfloat16)

    def send_columns(j):
        owner = j * stride

        @pl.when(s != owner)
        def _():
            remote(colbuf.at[j], colin.at[s], ksend.at[0], krecv.at[0], (owner, t)).start()

        @pl.when(s == owner)
        def _():
            colin[s] = colbuf[j]

    def knn_of(ref):
        best = absorb(lowest((4 * lanes, 128)), [ref[p].astype(jnp.float32) for p in range(ns)])
        mean = mean_of(fold_sublanes(best, (2, 1)))
        return jnp.concatenate([mean[4 * q + 3 : 4 * q + 4] for q in range(lanes)], axis=0)

    def mean_copy(k):
        j = s // stride
        return remote(ktown, kt_out.at[j], msend.at[0], mrecv.at[0], (lax.rem(s + k, ns), t))

    def merge_columns(j):
        @pl.when(s == j * stride)
        def _():
            ref = colin.at[pl.ds(0, ns - 1)]
            remote(ref, ref, ksend.at[0], krecv.at[0], core).wait_recv()
            ktown[...] = knn_of(colin)
            for k in range(1, ns):
                mean_copy(k).start()
            kt_out[j] = ktown[...]

    def within(j):
        return jnp.logical_and(j >= 0, j < first)

    def relay(to_side, there, behind_me, j):
        for d in range(1, nz):
            zp, present = behind_me(d)

            @pl.when(present)
            def _():
                to_side(j, zp).wait_recv()

                @pl.when(there)
                def _():
                    to_side(j, zp).start()

                to_over(j, zp).start()

    relays = (
        functools.partial(relay, to_left, has_left, lambda d: (z + d, z + d < nz)),
        functools.partial(relay, to_right, has_right, lambda d: (z - d, z - d >= 0)),
    )

    sides_both = (
        (both_left, has_left, HOP * z - depth, lambda d: (z + d, z + d < nz)),
        (both_right, has_right, -HOP * z, lambda d: (z - d, z - d >= 0)),
    )

    y_behind = depth + Y_LAG
    behind = y_behind + CORE_LAG

    def for_peers(what):
        for q in range(nz):
            zz = jnp.where(z < nz // 2, nz - 1 - q, q)
            for a in (1, 0):
                for b in (1, 0):
                    to = zz * 4 + lax.rem(y + a, 2) * 2 + lax.rem(c + b, 2)
                    if a or b:
                        what(to)
                    else:
                        pl.when(zz != z)(functools.partial(what, to))

    def tail_copy(e, to):
        src = colbuf.at[first - e]
        return remote(src, tailin.at[e, s], tsend.at[0], trecv.at[e], (to, t))

    def y_done(j):
        from_over(j).wait_recv()
        to_core(j, 1 - y).start()

    def tick(i, carry):
        for (to_side, there, lead), relay_side in zip(sides, relays):
            j = i + lead

            @pl.when(jnp.logical_and(within(j + z_ahead), there))
            def _():
                to_side(j + z_ahead, z, True).start()

            @pl.when(within(j))
            def _():
                relay_side(j)

        j = i - depth

        @pl.when(jnp.logical_and(j >= 0, j + y_ahead < first))
        def _():
            to_over(j + y_ahead, z, True).start()

        @pl.when(within(j))
        def _():
            to_core(j, y).start()

        m = i - behind
        jc = jnp.where(m == last, first, jnp.where(m == first, last, m))

        @pl.when(m == NORM_AT)
        def _():
            normalize_sources()

        @pl.when(m == last)
        def _():
            for which, slot in ((near, last), (pl.ds(far, 1), chunks)):
                ref = g.at[last, which, 1 - y, c]
                remote(ref, ref, ysend.at[0], yrecv.at[slot], over).wait_recv()
                ref = g.at[last, which, 1 - y, c]
                remote(ref, ref, csend.at[0], crecv.at[last], core).start()
            for j in range(last):
                merge_columns(j)

        @pl.when(m >= 0)
        def _():
            from_core(jc).wait_recv()
            compute(jc)


        @pl.when(jnp.logical_and(m >= 0, m < last))
        def _():
            send_columns(jc)

        @pl.when(m >= last)
        def _():
            for_peers(lambda to: tail_copy(m - last, to).start())
            tailin[m - last, s] = colbuf[jc]

        for both, there, lead, behind_me in sides_both:

            @pl.when(jnp.logical_and(i == first - lead - FIRST_LEAD, there))
            def _():
                both(z).start()

        final = last - 1 + behind
        for d in range(1, nz):
            for both, there, lead, behind_me in sides_both:
                zp, present = behind_me(d)
                at = jnp.where(there, jnp.minimum(first - lead + FIRST_GAP * (d - 1), final), final)

                @pl.when(jnp.logical_and(present, i == at))
                def _():
                    both(zp).wait_recv()

                    @pl.when(there)
                    def _():
                        both(zp).start()

        @pl.when(i == final)
        def _():
            to_core(first, y).start()
            to_core(first, 1 - y).start()

        jy = i - y_behind

        @pl.when(jnp.logical_and(jy >= 0, jy < last))
        def _():
            y_done(jy)

        return carry

    lax.fori_loop(0, chunks + behind, tick, 0)

    def row_copy(k):
        return remote(rowbuf, rowin.at[t], rsend.at[0], rrecv.at[0], (s, lax.rem(t + k, nt)))

    flat = [rowbest[k].T for k in range(4)]
    best = lowest((8, rows))
    for q in range(128 // 8):
        best = merge(best, tuple(flat[k][q * 8 : (q + 1) * 8, :] for k in range(4)))
    best = fold_sublanes(best)
    row = lax.broadcasted_iota(jnp.int32, (8, rows), 0)
    out = jnp.full((8, rows), -jnp.inf, jnp.float32)
    for k in range(4):
        out = jnp.where(row == k, best[k], out)
    rowbuf[...] = out
    rowin[t] = out
    for k in range(1, nt):
        row_copy(k).start()

    def drain_z(zp, kind, ref):
        @pl.when(jnp.logical_and(has_right, zp <= z))
        def _():
            remote(ref, ref, zsend.at[0, kind, zp], zrecv.at[0, zp], right).wait_send()

        @pl.when(jnp.logical_and(has_left, zp >= z))
        def _():
            remote(ref, ref, zsend.at[1, kind, zp], zrecv.at[0, zp], left).wait_send()

    for zp in range(nz):
        drain_z(zp, 0, g.at[pl.ds(0, first), 0, 0, 0])
        drain_z(zp, 1, g.at[0, 0, :, 0])
    ref = g.at[pl.ds(0, first), :, 0, 0]
    remote(ref, ref, ysend.at[0], yrecv.at[0], over).wait_send()
    swap(True).wait_send()
    ref = g.at[:, :, :, c]
    remote(ref, ref, csend.at[0], crecv.at[0], core).wait_send()
    for k in range(1, nt):
        to_tgt(k).wait_send()

    for e in range(2):
        ref = tailin.at[e, pl.ds(0, ns - 1)]
        remote(ref, ref, tsend.at[0], trecv.at[e], core).wait_recv()
        kt_out[first - e] = knn_of(tailin.at[e])
    for k in range(1, nt):
        row_copy(k).wait_send()
    ref = rowin.at[pl.ds(0, nt - 1)]
    remote(ref, ref, rsend.at[0], rrecv.at[0], core).wait_recv()
    half = 0.5 * mean_of(fold_sublanes(absorb(lowest((8, rows)), [rowin[p] for p in range(nt)])))
    ks_out[...] = jnp.broadcast_to(half[0:1], (128, rows)).T

    owns = jnp.logical_and(lax.rem(s, stride) == 0, s < last * stride)

    @pl.when(owns)
    def _():
        ref = colbuf.at[pl.ds(0, last - 1)]
        remote(ref, ref, ksend.at[0], krecv.at[0], core).wait_send()
        mean = kt_out.at[pl.ds(0, last - 1)]
        remote(mean, mean, msend.at[0], mrecv.at[0], core).wait_recv()
        for k in range(1, ns):
            mean_copy(k).wait_send()

    @pl.when(jnp.logical_not(owns))
    def _():
        ref = colbuf.at[pl.ds(0, last)]
        remote(ref, ref, ksend.at[0], krecv.at[0], core).wait_send()
        mean = kt_out.at[pl.ds(0, last)]
        remote(mean, mean, msend.at[0], mrecv.at[0], core).wait_recv()

    ref = tailin.at[:, pl.ds(0, ns - 1)]
    remote(ref, ref, tsend.at[0], trecv.at[0], core).wait_send()


def finish(s_ref, kt_ref, ks_ref, out_ref, half, held, sem):
    rows, cols = s_ref.shape
    tiles = cols // 128
    lanes = kt_ref.shape[1]
    for j in range(tiles):
        half[j] = jnp.broadcast_to(0.5 * kt_ref[j // lanes, j % lanes : j % lanes + 1, :], (8, 128))

    def block(b, carry):
        def at(h):
            return pl.ds(pl.multiple_of(b * BLOCK + 8 * h, 8), 8)

        mine = [ks_ref[at(h), :] for h in range(BLOCK // 8)]
        for q in range(tiles):
            lanes = slice(q * 128, (q + 1) * 128)
            other = half[q]
            for h in range(BLOCK // 8):
                v = s_ref[at(h), lanes]
                held[at(h), lanes] = jnp.where(v == excluded_score, jnp.float32(0.0), v / (mine[h] + other))
        span = pl.ds(pl.multiple_of(b * BLOCK, BLOCK), BLOCK)
        pltpu.make_async_copy(held.at[span], out_ref.at[span], sem.at[0]).start()
        return carry

    lax.fori_loop(0, rows // BLOCK, block, 0)
    pltpu.make_async_copy(held, out_ref, sem.at[0]).wait()


def body(ns, nt, src_emb, tgt_emb, src_ids, tgt_ids):
    rows, part = src_emb.shape
    cols, feats = tgt_emb.shape
    width = part * nt
    nz = ns // 4
    cw = min(CHUNK, cols)
    chunks = cols // cw
    lanes = cw // 128
    f32, bf16 = jnp.float32, jnp.bfloat16
    dma = pltpu.SemaphoreType.DMA
    hbm = pl.BlockSpec(memory_space=pltpu.MemorySpace.HBM)
    vmem = pl.BlockSpec(memory_space=pltpu.VMEM)
    args = (tgt_emb.T, src_emb, src_ids.reshape(1, rows), tgt_ids.reshape(1, cols))
    scores, kt, ks = pl.pallas_call(
        functools.partial(kernel, (ns, nt, nz, chunks, cw, feats)),
        out_shape=(
            jax.ShapeDtypeStruct((rows, cols), f32),
            jax.ShapeDtypeStruct((chunks, lanes, 128), f32),
            jax.ShapeDtypeStruct((rows, 128), f32),
        ),
        in_specs=[hbm, hbm, hbm, hbm],
        out_specs=(vmem, vmem, vmem),
        scratch_shapes=[
            pltpu.VMEM((1, rows), jnp.int32),
            pltpu.VMEM((1, cols), jnp.int32),
            pltpu.VMEM((rows, 128), jnp.int32),
            pltpu.VMEM((chunks, nz, 2, 2, feats, cw), bf16),
            pltpu.VMEM((rows, width), bf16),
            pltpu.VMEM((rows, width), bf16),
            pltpu.VMEM((rows, cw), f32),
            pltpu.VMEM((4, rows, 128), f32),
            pltpu.VMEM((chunks, 4 * lanes, 128), bf16),
            pltpu.VMEM((ns, 4 * lanes, 128), bf16),
            pltpu.VMEM((2, ns, 4 * lanes, 128), bf16),
            pltpu.VMEM((lanes, 128), f32),
            pltpu.VMEM((8, rows), f32),
            pltpu.VMEM((nt, 8, rows), f32),
            dma((chunks, nz)),
            dma((2, 2, nz)),
            dma((chunks + 1,)),
            dma((2,)),
            dma((chunks,)),
            dma((1,)),
            dma((nt,)),
            dma((1,)),
            dma((1,)),
            dma((1,)),
            dma((1,)),
            dma((1,)),
            dma((1,)),
            dma((1,)),
            dma((2,)),
            dma((1,)),
            dma((4,)),
        ],
        compiler_params=pltpu.CompilerParams(
            collective_id=0, has_side_effects=True, vmem_limit_bytes=40 * 2**20
        ),
    )(*(pltpu.with_memory_space_constraint(v, pltpu.MemorySpace.HBM) for v in args))
    return pl.pallas_call(
        finish,
        out_shape=jax.ShapeDtypeStruct((rows, cols), f32),
        in_specs=[vmem, vmem, vmem],
        out_specs=pl.BlockSpec(memory_space=pl.ANY),
        scratch_shapes=[
            pltpu.VMEM((cols // 128, 8, 128), f32),
            pltpu.VMEM((rows, cols), f32),
            dma((1,)),
        ],
        compiler_params=pltpu.CompilerParams(vmem_limit_bytes=40 * 2**20),
    )(scores, kt, ks)


def solution(mesh):
    return jax.shard_map(
        functools.partial(body, mesh.shape["src"], mesh.shape["tgt"]),
        mesh=mesh,
        in_specs=(P("src", "tgt"), P("tgt", "src"), P("src"), P("tgt")),
        out_specs=P("src", "tgt"),
        check_vma=False,
    )
```

```python
import functools

import jax
import jax.numpy as jnp
from jax import lax
from jax.experimental import pallas as pl
from jax.experimental.pallas import tpu as pltpu
from jax.sharding import PartitionSpec as P

epsilon = 1e-06
excluded_score = -2.0
MESH = pl.DeviceIdType.MESH
CHUNK = 512
FIRST_LEAD = 1
FIRST_GAP = 1
Z_AHEAD = 3
Y_AHEAD = 7
BLOCK = 32
HOP = 1
Y_LAG = 2
CORE_LAG = 1
NORM_AT = -1


def sort4(v):
    a, b = jnp.maximum(v[0], v[1]), jnp.minimum(v[0], v[1])
    c, d = jnp.maximum(v[2], v[3]), jnp.minimum(v[2], v[3])
    top, e = jnp.maximum(a, c), jnp.minimum(a, c)
    f, low = jnp.maximum(b, d), jnp.minimum(b, d)
    return (top, jnp.maximum(e, f), jnp.minimum(e, f), low)


def merge(first, second):
    c = [jnp.maximum(first[k], second[3 - k]) for k in range(4)]
    a, b = jnp.maximum(c[0], c[2]), jnp.maximum(c[1], c[3])
    d, e = jnp.minimum(c[0], c[2]), jnp.minimum(c[1], c[3])
    return (jnp.maximum(a, b), jnp.minimum(a, b), jnp.maximum(d, e), jnp.minimum(d, e))


def insert(best, value):
    out = []
    for level in best[:-1]:
        out.append(jnp.maximum(level, value))
        value = jnp.minimum(level, value)
    out.append(jnp.maximum(best[-1], value))
    return tuple(out)


def absorb(best, values):
    whole = len(values) // 4 * 4
    for k in range(0, whole, 4):
        best = merge(best, sort4(values[k : k + 4]))
    for value in values[whole:]:
        best = insert(best, value)
    return best


def fold_sublanes(best, shifts=(4, 2, 1)):
    for shift in shifts:
        best = merge(best, tuple(pltpu.roll(level, shift, 0) for level in best))
    return best


def mean_of(best):
    return (best[0] + best[1] + best[2] + best[3]) * 0.25


def lowest(shape):
    return tuple(jnp.full(shape, -jnp.inf, jnp.float32) for _ in range(4))


def kernel(dims, x_ref, a_ref, sid_ref, tid_ref, s_out, kt_out, ks_out, sid, tid, sids, g, a_whole, a_unit, raw, rowbest,
           colbuf, colin, tailin, lineown, linein, ktown, rowbuf, rowin, zrecv, zsend, yrecv, ysend, crecv, csend, arecv, asend, rrecv,
           rsend, krecv, ksend, mrecv, msend, trecv, tsend, osend, orecv, lsem):
    ns, nt, nz, chunks, cw, feats = dims
    s = lax.axis_index("src")
    t = lax.axis_index("tgt")
    z, y, c = s // 4, (s // 2) % 2, s % 2
    right = (s + 4, t)
    left = (s - 4, t)
    over = (z * 4 + (1 - y) * 2 + c, t)
    core = (s + 1 - 2 * c, t)
    rows, width = a_unit.shape
    part = a_ref.shape[1]
    lanes = cw // 128
    first = chunks - 1
    last = first - 1
    has_right, has_left = z + 1 < nz, z >= 1

    def remote(src, dst, send, recv, where):
        return pltpu.make_async_remote_copy(
            src_ref=src, dst_ref=dst, send_sem=send, recv_sem=recv, device_id=where, device_id_type=MESH
        )

    def chunk_cols(j):
        return pl.ds(pl.multiple_of(j * cw, cw), cw)

    barrier = pltpu.get_barrier_semaphore()

    @pl.when(has_right)
    def _():
        pl.semaphore_signal(barrier, inc=1, device_id=right, device_id_type=MESH)

    @pl.when(has_left)
    def _():
        pl.semaphore_signal(barrier, inc=1, device_id=left, device_id_type=MESH)

    pl.semaphore_signal(barrier, inc=1, device_id=over, device_id_type=MESH)
    pl.semaphore_signal(barrier, inc=1, device_id=core, device_id_type=MESH)
    for k in range(1, nt):
        pl.semaphore_signal(barrier, inc=1, device_id=(s, lax.rem(t + k, nt)), device_id_type=MESH)

    for j in range(chunks):
        pltpu.make_async_copy(x_ref.at[:, chunk_cols(j)], g.at[j, z, y, c], lsem.at[0]).start()
    acols = pl.ds(pl.multiple_of(t * part, part), part)
    local_a = pltpu.make_async_copy(a_ref, a_whole.at[:, acols], lsem.at[1])
    local_sid = pltpu.make_async_copy(sid_ref, sid, lsem.at[2])
    local_tid = pltpu.make_async_copy(tid_ref, tid, lsem.at[3])
    local_a.start()
    local_sid.start()
    local_tid.start()
    pl.semaphore_wait(barrier, 1 + nt + has_right.astype(jnp.int32) + has_left.astype(jnp.int32))

    def to_right(j, zp, own=False):
        ref = g.at[j, zp, y, c]
        return remote(x_ref.at[:, chunk_cols(j)] if own else ref, ref, zsend.at[0, 0, zp], zrecv.at[j, zp], right)

    def to_left(j, zp, own=False):
        ref = g.at[j, zp, y, c]
        return remote(x_ref.at[:, chunk_cols(j)] if own else ref, ref, zsend.at[1, 0, zp], zrecv.at[j, zp], left)

    def both_right(zp):
        ref = g.at[first, zp, :, c]
        return remote(ref, ref, zsend.at[0, 1, zp], zrecv.at[first, zp], right)

    def both_left(zp):
        ref = g.at[first, zp, :, c]
        return remote(ref, ref, zsend.at[1, 1, zp], zrecv.at[first, zp], left)

    far = jnp.where(z < nz // 2, nz - 1, 0)
    near = pl.ds(jnp.where(z < nz // 2, 0, 1), nz - 1)

    def to_over(j, zp, own=False):
        ref = g.at[j, zp, y, c]
        src = x_ref.at[:, chunk_cols(j)] if own else ref
        slot = jnp.where(jnp.logical_and(j == last, zp == far), chunks, j)
        return remote(src, ref, ysend.at[0], yrecv.at[slot], over)

    def from_over(j):
        ref = g.at[j, :, 1 - y, c]
        return remote(ref, ref, ysend.at[0], yrecv.at[j], over)

    def swap(own):
        ref = g.at[first, z, y, c] if own else g.at[first, z, 1 - y, c]
        return remote(x_ref.at[:, chunk_cols(first)] if own else ref, ref, ysend.at[1], yrecv.at[first], over)

    def to_core(j, yy):
        ref = g.at[j, :, yy, c]
        return remote(ref, ref, csend.at[0], crecv.at[j], core)

    def from_core(j):
        ref = g.at[j, :, :, 1 - c]
        return remote(ref, ref, csend.at[0], crecv.at[j], core)

    def to_tgt(k):
        return remote(a_ref, a_whole.at[:, acols], asend.at[0], arecv.at[t], (s, lax.rem(t + k, nt)))

    z_ahead, y_ahead = min(Z_AHEAD, first - 1), min(Y_AHEAD, first)
    depth = HOP * (nz - 1)
    sides = ((to_left, has_left, HOP * z - depth), (to_right, has_right, -HOP * z))
    swap(True).start()
    for j in range(max(y_ahead, z_ahead)):
        if j < y_ahead:
            to_over(j, z, True).start()
        if j < z_ahead:
            for to_side, there, lead in sides:

                @pl.when(jnp.logical_and(there, j < lead + z_ahead))
                def _():
                    to_side(j, z, True).start()

    for k in range(1, nt):
        to_tgt(k).start()
    pltpu.make_async_copy(g.at[:, z, y, c], g.at[:, z, y, c], lsem.at[0]).wait()
    swap(False).wait_recv()
    local_sid.wait()
    local_tid.wait()
    sids[...] = jnp.broadcast_to(sid[...], (128, rows)).T
    for k in range(4):
        rowbest[k] = jnp.full(rowbest.shape[1:], -jnp.inf, jnp.float32)

    def normalize_sources():
        local_a.wait()
        for k in range(1, nt):
            other = lax.rem(t + k, nt)
            cols = pl.ds(pl.multiple_of(other * part, part), part)
            remote(a_ref, a_whole.at[:, cols], asend.at[0], arecv.at[other], (s, other)).wait_recv()
        block = 16

        def step(r, carry):
            at = pl.ds(pl.multiple_of(r * block, block), block)
            v = a_whole[at, :].astype(jnp.float32)
            scale = jnp.sqrt(jnp.sum(v * v, axis=1, keepdims=True) + epsilon)
            a_unit[at, :] = (v / scale).astype(jnp.bfloat16)
            return carry

        lax.fori_loop(0, rows // block, step, 0, unroll=2)

    def compute(j):
        cols = chunk_cols(j)
        found = g[j].reshape(width, cw)
        raw[...] = jnp.dot(a_unit[...], found, preferred_element_type=jnp.float32)
        found = found.astype(jnp.float32)
        acc = jnp.sum((found * found).reshape(width // 8, 8, cw), axis=0)
        inverse = jnp.broadcast_to(1.0 / jnp.sqrt(jnp.sum(acc, axis=0, keepdims=True) + epsilon), (8, cw))
        tids = jnp.broadcast_to(tid[:, cols], (8, cw))

        def group(r, best):
            ats = [pl.ds(pl.multiple_of(r * 32 + h * 8, 8), 8) for h in range(4)]
            spans = [slice(q * 128, (q + 1) * 128) for q in range(lanes)]
            ids = [sids[at, :] for at in ats]
            found = [[raw[at, span] for span in spans] for at in ats]
            rows_in = [tuple(rowbest[k, at, :] for k in range(4)) for at in ats]
            found = [
                [jnp.where(ids[h] == tids[:, span], jnp.float32(excluded_score), v * inverse[:, span]) for v, span in zip(found[h], spans)]
                for h in range(4)
            ]
            rows_out = [absorb(rows_in[h], found[h]) for h in range(4)]
            best = tuple(absorb(best[q], [found[h][q] for h in range(4)]) for q in range(lanes))
            for h, at in enumerate(ats):
                for q in range(lanes):
                    s_out[at, pl.ds(pl.multiple_of(j * cw + q * 128, 128), 128)] = found[h][q]
                for k in range(4):
                    rowbest[k, at, :] = rows_out[h][k]
            return best

        best = lax.fori_loop(0, rows // 32, group, tuple(lowest((8, 128)) for _ in range(lanes)), unroll=1)
        best = [fold_sublanes(b) for b in best]
        row = lax.broadcasted_iota(jnp.int32, (8, 128), 0)
        tiles = []
        for q in range(0, lanes, 2):
            out = best[q][0]
            for k in range(1, 8):
                out = jnp.where(row == k, best[q + k // 4][k % 4], out)
            tiles.append(out)
        colbuf[j] = jnp.concatenate(tiles, axis=0).astype(jnp.bfloat16)

    mine = z * 2 + c
    share = 2 * nz // chunks

    def line(i):
        return (i // 2 * 4 + y * 2 + lax.rem(i, 2), t)

    def send_columns(j):
        @pl.when(mine != j * share)
        def _():
            remote(colbuf.at[j], colin.at[mine], ksend.at[0], krecv.at[0], line(j * share)).start()

        @pl.when(mine == j * share)
        def _():
            colin[mine] = colbuf[j]

    owns = jnp.logical_and(lax.rem(mine, share) == 0, mine < last * share)

    def knn_of(ref):
        best = absorb(lowest((4 * lanes, 128)), [ref[p].astype(jnp.float32) for p in range(ns)])
        mean = mean_of(fold_sublanes(best, (2, 1)))
        return jnp.concatenate([mean[4 * q + 3 : 4 * q + 4] for q in range(lanes)], axis=0)

    def line_copy():
        return remote(lineown, linein, osend.at[0], orecv.at[0], over)

    def mean_copy(k):
        return remote(ktown, kt_out.at[mine // share], msend.at[0], mrecv.at[0], line(lax.rem(mine + k, 2 * nz)))

    def merge_line():
        @pl.when(owns)
        def _():
            ref = colin.at[pl.ds(0, 2 * nz - 1)]
            remote(ref, ref, ksend.at[0], krecv.at[0], core).wait_recv()
            best = absorb(lowest((4 * lanes, 128)), [colin[p].astype(jnp.float32) for p in range(2 * nz)])
            best = fold_sublanes(best, (2, 1))
            row = lax.rem(lax.broadcasted_iota(jnp.int32, (4 * lanes, 128), 0), 4)
            out = best[3]
            for k in range(3):
                out = jnp.where(row == k, pltpu.roll(best[k], 4 * lanes - 3 + k, 0), out)
            lineown[...] = out.astype(jnp.bfloat16)
            line_copy().start()

    def merge_columns():
        @pl.when(owns)
        def _():
            line_copy().wait_recv()
            ours, theirs = lineown[...].astype(jnp.float32), linein[...].astype(jnp.float32)
            best = fold_sublanes(insert(insert(lowest((4 * lanes, 128)), ours), theirs), (2, 1))
            mean = mean_of(best)
            ktown[...] = jnp.concatenate([mean[4 * q + 3 : 4 * q + 4] for q in range(lanes)], axis=0)
            for k in range(1, 2 * nz):
                mean_copy(k).start()
            kt_out[mine // share] = ktown[...]

    def within(j):
        return jnp.logical_and(j >= 0, j < first)

    def relay(to_side, there, behind_me, j):
        for d in range(1, nz):
            zp, present = behind_me(d)

            @pl.when(present)
            def _():
                to_side(j, zp).wait_recv()

                @pl.when(there)
                def _():
                    to_side(j, zp).start()

                to_over(j, zp).start()

    relays = (
        functools.partial(relay, to_left, has_left, lambda d: (z + d, z + d < nz)),
        functools.partial(relay, to_right, has_right, lambda d: (z - d, z - d >= 0)),
    )

    sides_both = (
        (both_left, has_left, HOP * z - depth, lambda d: (z + d, z + d < nz)),
        (both_right, has_right, -HOP * z, lambda d: (z - d, z - d >= 0)),
    )

    y_behind = depth + Y_LAG
    behind = y_behind + CORE_LAG

    def for_peers(what):
        for q in range(nz):
            zz = jnp.where(z < nz // 2, nz - 1 - q, q)
            for a in (1, 0):
                for b in (1, 0):
                    to = zz * 4 + lax.rem(y + a, 2) * 2 + lax.rem(c + b, 2)
                    if a or b:
                        what(to)
                    else:
                        pl.when(zz != z)(functools.partial(what, to))

    def tail_copy(e, to):
        src = colbuf.at[first - e]
        return remote(src, tailin.at[e, s], tsend.at[0], trecv.at[e], (to, t))

    def y_done(j):
        from_over(j).wait_recv()
        to_core(j, 1 - y).start()

    def tick(i, carry):
        for (to_side, there, lead), relay_side in zip(sides, relays):
            j = i + lead

            @pl.when(jnp.logical_and(within(j + z_ahead), there))
            def _():
                to_side(j + z_ahead, z, True).start()

            @pl.when(within(j))
            def _():
                relay_side(j)

        j = i - depth

        @pl.when(jnp.logical_and(j >= 0, j + y_ahead < first))
        def _():
            to_over(j + y_ahead, z, True).start()

        @pl.when(within(j))
        def _():
            to_core(j, y).start()

        m = i - behind
        jc = jnp.where(m == last, first, jnp.where(m == first, last, m))

        @pl.when(m == NORM_AT)
        def _():
            normalize_sources()

        @pl.when(m == last)
        def _():
            for which, slot in ((near, last), (pl.ds(far, 1), chunks)):
                ref = g.at[last, which, 1 - y, c]
                remote(ref, ref, ysend.at[0], yrecv.at[slot], over).wait_recv()
                ref = g.at[last, which, 1 - y, c]
                remote(ref, ref, csend.at[0], crecv.at[last], core).start()
            merge_line()

        @pl.when(m >= 0)
        def _():
            from_core(jc).wait_recv()
            compute(jc)


        @pl.when(jnp.logical_and(m >= 0, m < last))
        def _():
            send_columns(jc)

        @pl.when(m >= last)
        def _():
            for_peers(lambda to: tail_copy(m - last, to).start())
            tailin[m - last, s] = colbuf[jc]

        for both, there, lead, behind_me in sides_both:

            @pl.when(jnp.logical_and(i == first - lead - FIRST_LEAD, there))
            def _():
                both(z).start()

        final = last - 1 + behind
        for d in range(1, nz):
            for both, there, lead, behind_me in sides_both:
                zp, present = behind_me(d)
                at = jnp.where(there, jnp.minimum(first - lead + FIRST_GAP * (d - 1), final), final)

                @pl.when(jnp.logical_and(present, i == at))
                def _():
                    both(zp).wait_recv()

                    @pl.when(there)
                    def _():
                        both(zp).start()

        @pl.when(i == final)
        def _():
            to_core(first, y).start()
            to_core(first, 1 - y).start()

        jy = i - y_behind

        @pl.when(jnp.logical_and(jy >= 0, jy < last))
        def _():
            y_done(jy)

        return carry

    lax.fori_loop(0, chunks + behind, tick, 0)

    def row_copy(k):
        return remote(rowbuf, rowin.at[t], rsend.at[0], rrecv.at[0], (s, lax.rem(t + k, nt)))

    flat = [rowbest[k].T for k in range(4)]
    best = lowest((8, rows))
    for q in range(128 // 8):
        best = merge(best, tuple(flat[k][q * 8 : (q + 1) * 8, :] for k in range(4)))
    best = fold_sublanes(best)
    row = lax.broadcasted_iota(jnp.int32, (8, rows), 0)
    out = jnp.full((8, rows), -jnp.inf, jnp.float32)
    for k in range(4):
        out = jnp.where(row == k, best[k], out)
    rowbuf[...] = out
    rowin[t] = out
    for k in range(1, nt):
        row_copy(k).start()
    merge_columns()

    def drain_z(zp, kind, ref):
        @pl.when(jnp.logical_and(has_right, zp <= z))
        def _():
            remote(ref, ref, zsend.at[0, kind, zp], zrecv.at[0, zp], right).wait_send()

        @pl.when(jnp.logical_and(has_left, zp >= z))
        def _():
            remote(ref, ref, zsend.at[1, kind, zp], zrecv.at[0, zp], left).wait_send()

    for zp in range(nz):
        drain_z(zp, 0, g.at[pl.ds(0, first), 0, 0, 0])
        drain_z(zp, 1, g.at[0, 0, :, 0])
    ref = g.at[pl.ds(0, first), :, 0, 0]
    remote(ref, ref, ysend.at[0], yrecv.at[0], over).wait_send()
    swap(True).wait_send()
    ref = g.at[:, :, :, c]
    remote(ref, ref, csend.at[0], crecv.at[0], core).wait_send()
    for k in range(1, nt):
        to_tgt(k).wait_send()

    def tail_done(e):
        ref = tailin.at[e, pl.ds(0, ns - 1)]
        remote(ref, ref, tsend.at[0], trecv.at[e], core).wait_recv()
        kt_out[first - e] = knn_of(tailin.at[e])

    tail_done(0)
    for k in range(1, nt):
        row_copy(k).wait_send()
    ref = rowin.at[pl.ds(0, nt - 1)]
    remote(ref, ref, rsend.at[0], rrecv.at[0], core).wait_recv()
    half = 0.5 * mean_of(fold_sublanes(absorb(lowest((8, rows)), [rowin[p] for p in range(nt)])))
    ks_out[...] = jnp.broadcast_to(half[0:1], (128, rows)).T
    tail_done(1)
    @pl.when(owns)
    def _():
        ref = colbuf.at[pl.ds(0, last - 1)]
        remote(ref, ref, ksend.at[0], krecv.at[0], core).wait_send()
        mean = kt_out.at[pl.ds(0, last - 1)]
        remote(mean, mean, msend.at[0], mrecv.at[0], core).wait_recv()
        for k in range(1, 2 * nz):
            mean_copy(k).wait_send()
        line_copy().wait_send()

    @pl.when(jnp.logical_not(owns))
    def _():
        ref = colbuf.at[pl.ds(0, last)]
        remote(ref, ref, ksend.at[0], krecv.at[0], core).wait_send()
        mean = kt_out.at[pl.ds(0, last)]
        remote(mean, mean, msend.at[0], mrecv.at[0], core).wait_recv()

    ref = tailin.at[:, pl.ds(0, ns - 1)]
    remote(ref, ref, tsend.at[0], trecv.at[0], core).wait_send()


def finish(s_ref, kt_ref, ks_ref, out_ref, half, held, sem):
    rows, cols = s_ref.shape
    tiles = cols // 128
    lanes = kt_ref.shape[1]
    for j in range(tiles):
        half[j] = jnp.broadcast_to(0.5 * kt_ref[j // lanes, j % lanes : j % lanes + 1, :], (8, 128))

    def block(b, carry):
        def at(h):
            return pl.ds(pl.multiple_of(b * BLOCK + 8 * h, 8), 8)

        mine = [ks_ref[at(h), :] for h in range(BLOCK // 8)]
        for q in range(tiles):
            lanes = slice(q * 128, (q + 1) * 128)
            other = half[q]
            for h in range(BLOCK // 8):
                v = s_ref[at(h), lanes]
                held[at(h), lanes] = jnp.where(v == excluded_score, jnp.float32(0.0), v / (mine[h] + other))
        span = pl.ds(pl.multiple_of(b * BLOCK, BLOCK), BLOCK)
        pltpu.make_async_copy(held.at[span], out_ref.at[span], sem.at[0]).start()
        return carry

    lax.fori_loop(0, rows // BLOCK, block, 0)
    pltpu.make_async_copy(held, out_ref, sem.at[0]).wait()


def body(ns, nt, src_emb, tgt_emb, src_ids, tgt_ids):
    rows, part = src_emb.shape
    cols, feats = tgt_emb.shape
    width = part * nt
    nz = ns // 4
    cw = min(CHUNK, cols)
    chunks = cols // cw
    lanes = cw // 128
    f32, bf16 = jnp.float32, jnp.bfloat16
    dma = pltpu.SemaphoreType.DMA
    hbm = pl.BlockSpec(memory_space=pltpu.MemorySpace.HBM)
    vmem = pl.BlockSpec(memory_space=pltpu.VMEM)
    args = (tgt_emb.T, src_emb, src_ids.reshape(1, rows), tgt_ids.reshape(1, cols))
    scores, kt, ks = pl.pallas_call(
        functools.partial(kernel, (ns, nt, nz, chunks, cw, feats)),
        out_shape=(
            jax.ShapeDtypeStruct((rows, cols), f32),
            jax.ShapeDtypeStruct((chunks, lanes, 128), f32),
            jax.ShapeDtypeStruct((rows, 128), f32),
        ),
        in_specs=[hbm, hbm, hbm, hbm],
        out_specs=(vmem, vmem, vmem),
        scratch_shapes=[
            pltpu.VMEM((1, rows), jnp.int32),
            pltpu.VMEM((1, cols), jnp.int32),
            pltpu.VMEM((rows, 128), jnp.int32),
            pltpu.VMEM((chunks, nz, 2, 2, feats, cw), bf16),
            pltpu.VMEM((rows, width), bf16),
            pltpu.VMEM((rows, width), bf16),
            pltpu.VMEM((rows, cw), f32),
            pltpu.VMEM((4, rows, 128), f32),
            pltpu.VMEM((chunks, 4 * lanes, 128), bf16),
            pltpu.VMEM((ns, 4 * lanes, 128), bf16),
            pltpu.VMEM((2, ns, 4 * lanes, 128), bf16),
            pltpu.VMEM((4 * lanes, 128), bf16),
            pltpu.VMEM((4 * lanes, 128), bf16),
            pltpu.VMEM((lanes, 128), f32),
            pltpu.VMEM((8, rows), f32),
            pltpu.VMEM((nt, 8, rows), f32),
            dma((chunks, nz)),
            dma((2, 2, nz)),
            dma((chunks + 1,)),
            dma((2,)),
            dma((chunks,)),
            dma((1,)),
            dma((nt,)),
            dma((1,)),
            dma((1,)),
            dma((1,)),
            dma((1,)),
            dma((1,)),
            dma((1,)),
            dma((1,)),
            dma((2,)),
            dma((1,)),
            dma((1,)),
            dma((1,)),
            dma((4,)),
        ],
        compiler_params=pltpu.CompilerParams(
            collective_id=0, has_side_effects=True, vmem_limit_bytes=40 * 2**20
        ),
    )(*(pltpu.with_memory_space_constraint(v, pltpu.MemorySpace.HBM) for v in args))
    return pl.pallas_call(
        finish,
        out_shape=jax.ShapeDtypeStruct((rows, cols), f32),
        in_specs=[vmem, vmem, vmem],
        out_specs=pl.BlockSpec(memory_space=pl.ANY),
        scratch_shapes=[
            pltpu.VMEM((cols // 128, 8, 128), f32),
            pltpu.VMEM((rows, cols), f32),
            dma((1,)),
        ],
        compiler_params=pltpu.CompilerParams(vmem_limit_bytes=40 * 2**20),
    )(scores, kt, ks)


def solution(mesh):
    return jax.shard_map(
        functools.partial(body, mesh.shape["src"], mesh.shape["tgt"]),
        mesh=mesh,
        in_specs=(P("src", "tgt"), P("tgt", "src"), P("src"), P("tgt")),
        out_specs=P("src", "tgt"),
        check_vma=False,
    )
```

```python
import functools

import jax
import jax.numpy as jnp
from jax import lax
from jax.experimental import pallas as pl
from jax.experimental.pallas import tpu as pltpu
from jax.sharding import PartitionSpec as P

epsilon = 1e-06
excluded_score = -2.0
MESH = pl.DeviceIdType.MESH
CHUNK = 512
FIRST_LEAD = 1
FIRST_GAP = 1
Z_AHEAD = 3
Y_AHEAD = 7
BLOCK = 32
HOP = 1
Y_LAG = 2
CORE_LAG = 1
NORM_AT = -1


def sort4(v):
    a, b = jnp.maximum(v[0], v[1]), jnp.minimum(v[0], v[1])
    c, d = jnp.maximum(v[2], v[3]), jnp.minimum(v[2], v[3])
    top, e = jnp.maximum(a, c), jnp.minimum(a, c)
    f, low = jnp.maximum(b, d), jnp.minimum(b, d)
    return (top, jnp.maximum(e, f), jnp.minimum(e, f), low)


def merge(first, second):
    c = [jnp.maximum(first[k], second[3 - k]) for k in range(4)]
    a, b = jnp.maximum(c[0], c[2]), jnp.maximum(c[1], c[3])
    d, e = jnp.minimum(c[0], c[2]), jnp.minimum(c[1], c[3])
    return (jnp.maximum(a, b), jnp.minimum(a, b), jnp.maximum(d, e), jnp.minimum(d, e))


def insert(best, value):
    out = []
    for level in best[:-1]:
        out.append(jnp.maximum(level, value))
        value = jnp.minimum(level, value)
    out.append(jnp.maximum(best[-1], value))
    return tuple(out)


def absorb(best, values):
    whole = len(values) // 4 * 4
    for k in range(0, whole, 4):
        best = merge(best, sort4(values[k : k + 4]))
    for value in values[whole:]:
        best = insert(best, value)
    return best


def fold_sublanes(best, shifts=(4, 2, 1)):
    for shift in shifts:
        best = merge(best, tuple(pltpu.roll(level, shift, 0) for level in best))
    return best


def mean_of(best):
    return (best[0] + best[1] + best[2] + best[3]) * 0.25


def lowest(shape):
    return tuple(jnp.full(shape, -jnp.inf, jnp.float32) for _ in range(4))


def kernel(dims, x_ref, a_ref, sid_ref, tid_ref, s_out, kt_out, ks_out, sid, tid, sids, g, a_whole, a_unit, raw, rowbest,
           colbuf, colin, tailin, lineown, linein, ktown, rowbuf, rowin, zrecv, zsend, yrecv, ysend, crecv, csend, arecv, asend, rrecv,
           rsend, krecv, ksend, mrecv, msend, trecv, tsend, osend, orecv, lsem):
    ns, nt, nz, chunks, cw, feats = dims
    s = lax.axis_index("src")
    t = lax.axis_index("tgt")
    z, y, c = s // 4, (s // 2) % 2, s % 2
    right = (s + 4, t)
    left = (s - 4, t)
    over = (z * 4 + (1 - y) * 2 + c, t)
    core = (s + 1 - 2 * c, t)
    rows, width = a_unit.shape
    part = a_ref.shape[1]
    lanes = cw // 128
    first = chunks - 1
    last = first - 1
    has_right, has_left = z + 1 < nz, z >= 1

    def remote(src, dst, send, recv, where):
        return pltpu.make_async_remote_copy(
            src_ref=src, dst_ref=dst, send_sem=send, recv_sem=recv, device_id=where, device_id_type=MESH
        )

    def chunk_cols(j):
        return pl.ds(pl.multiple_of(j * cw, cw), cw)

    barrier = pltpu.get_barrier_semaphore()

    @pl.when(has_right)
    def _():
        pl.semaphore_signal(barrier, inc=1, device_id=right, device_id_type=MESH)

    @pl.when(has_left)
    def _():
        pl.semaphore_signal(barrier, inc=1, device_id=left, device_id_type=MESH)

    pl.semaphore_signal(barrier, inc=1, device_id=over, device_id_type=MESH)
    pl.semaphore_signal(barrier, inc=1, device_id=core, device_id_type=MESH)
    for k in range(1, nt):
        pl.semaphore_signal(barrier, inc=1, device_id=(s, lax.rem(t + k, nt)), device_id_type=MESH)

    for j in range(chunks):
        pltpu.make_async_copy(x_ref.at[:, chunk_cols(j)], g.at[j, z, y, c], lsem.at[0]).start()
    acols = pl.ds(pl.multiple_of(t * part, part), part)
    local_a = pltpu.make_async_copy(a_ref, a_whole.at[:, acols], lsem.at[1])
    local_sid = pltpu.make_async_copy(sid_ref, sid, lsem.at[2])
    local_tid = pltpu.make_async_copy(tid_ref, tid, lsem.at[3])
    local_a.start()
    local_sid.start()
    local_tid.start()
    pl.semaphore_wait(barrier, 1 + nt + has_right.astype(jnp.int32) + has_left.astype(jnp.int32))

    def to_right(j, zp, own=False):
        ref = g.at[j, zp, y, c]
        return remote(x_ref.at[:, chunk_cols(j)] if own else ref, ref, zsend.at[0, 0], zrecv.at[j, zp], right)

    def to_left(j, zp, own=False):
        ref = g.at[j, zp, y, c]
        return remote(x_ref.at[:, chunk_cols(j)] if own else ref, ref, zsend.at[1, 0], zrecv.at[j, zp], left)

    def both_right(zp):
        ref = g.at[first, zp, :, c]
        return remote(ref, ref, zsend.at[0, 1], zrecv.at[first, zp], right)

    def both_left(zp):
        ref = g.at[first, zp, :, c]
        return remote(ref, ref, zsend.at[1, 1], zrecv.at[first, zp], left)

    far = jnp.where(z < nz // 2, nz - 1, 0)
    near = pl.ds(jnp.where(z < nz // 2, 0, 1), nz - 1)

    def to_over(j, zp, own=False):
        ref = g.at[j, zp, y, c]
        src = x_ref.at[:, chunk_cols(j)] if own else ref
        slot = jnp.where(jnp.logical_and(j == last, zp == far), chunks, j)
        return remote(src, ref, ysend.at[0], yrecv.at[slot], over)

    def from_over(j):
        ref = g.at[j, :, 1 - y, c]
        return remote(ref, ref, ysend.at[0], yrecv.at[j], over)

    def swap(own):
        ref = g.at[first, z, y, c] if own else g.at[first, z, 1 - y, c]
        return remote(x_ref.at[:, chunk_cols(first)] if own else ref, ref, ysend.at[1], yrecv.at[first], over)

    def to_core(j, yy):
        ref = g.at[j, :, yy, c]
        return remote(ref, ref, csend.at[0], crecv.at[j], core)

    def from_core(j):
        ref = g.at[j, :, :, 1 - c]
        return remote(ref, ref, csend.at[0], crecv.at[j], core)

    def to_tgt(k):
        return remote(a_ref, a_whole.at[:, acols], asend.at[0], arecv.at[t], (s, lax.rem(t + k, nt)))

    z_ahead, y_ahead = min(Z_AHEAD, first - 1), min(Y_AHEAD, first)
    depth = HOP * (nz - 1)
    sides = ((to_left, has_left, HOP * z - depth), (to_right, has_right, -HOP * z))
    swap(True).start()
    for j in range(max(y_ahead, z_ahead)):
        if j < y_ahead:
            to_over(j, z, True).start()
        if j < z_ahead:
            for to_side, there, lead in sides:

                @pl.when(jnp.logical_and(there, j < lead + z_ahead))
                def _():
                    to_side(j, z, True).start()

    for k in range(1, nt):
        to_tgt(k).start()
    pltpu.make_async_copy(g.at[:, z, y, c], g.at[:, z, y, c], lsem.at[0]).wait()
    swap(False).wait_recv()
    local_sid.wait()
    local_tid.wait()
    sids[...] = jnp.broadcast_to(sid[...], (128, rows)).T
    for k in range(4):
        rowbest[k] = jnp.full(rowbest.shape[1:], -jnp.inf, jnp.float32)

    def normalize_sources():
        local_a.wait()
        for k in range(1, nt):
            other = lax.rem(t + k, nt)
            cols = pl.ds(pl.multiple_of(other * part, part), part)
            remote(a_ref, a_whole.at[:, cols], asend.at[0], arecv.at[other], (s, other)).wait_recv()
        block = 16

        def step(r, carry):
            at = pl.ds(pl.multiple_of(r * block, block), block)
            v = a_whole[at, :].astype(jnp.float32)
            scale = jnp.sqrt(jnp.sum(v * v, axis=1, keepdims=True) + epsilon)
            a_unit[at, :] = (v / scale).astype(jnp.bfloat16)
            return carry

        lax.fori_loop(0, rows // block, step, 0, unroll=2)

    def compute(j):
        cols = chunk_cols(j)
        found = g[j].reshape(width, cw)
        raw[...] = jnp.dot(a_unit[...], found, preferred_element_type=jnp.float32)
        found = found.astype(jnp.float32)
        acc = jnp.sum((found * found).reshape(width // 8, 8, cw), axis=0)
        inverse = jnp.broadcast_to(1.0 / jnp.sqrt(jnp.sum(acc, axis=0, keepdims=True) + epsilon), (8, cw))
        tids = jnp.broadcast_to(tid[:, cols], (8, cw))

        def group(r, best):
            ats = [pl.ds(pl.multiple_of(r * 32 + h * 8, 8), 8) for h in range(4)]
            spans = [slice(q * 128, (q + 1) * 128) for q in range(lanes)]
            ids = [sids[at, :] for at in ats]
            found = [[raw[at, span] for span in spans] for at in ats]
            rows_in = [tuple(rowbest[k, at, :] for k in range(4)) for at in ats]
            found = [
                [jnp.where(ids[h] == tids[:, span], jnp.float32(excluded_score), v * inverse[:, span]) for v, span in zip(found[h], spans)]
                for h in range(4)
            ]
            rows_out = [absorb(rows_in[h], found[h]) for h in range(4)]
            best = tuple(absorb(best[q], [found[h][q] for h in range(4)]) for q in range(lanes))
            for h, at in enumerate(ats):
                for q in range(lanes):
                    s_out[at, pl.ds(pl.multiple_of(j * cw + q * 128, 128), 128)] = found[h][q]
                for k in range(4):
                    rowbest[k, at, :] = rows_out[h][k]
            return best

        best = lax.fori_loop(0, rows // 32, group, tuple(lowest((8, 128)) for _ in range(lanes)), unroll=2)
        best = [fold_sublanes(b) for b in best]
        row = lax.broadcasted_iota(jnp.int32, (8, 128), 0)
        tiles = []
        for q in range(0, lanes, 2):
            out = best[q][0]
            for k in range(1, 8):
                out = jnp.where(row == k, best[q + k // 4][k % 4], out)
            tiles.append(out)
        colbuf[j] = jnp.concatenate(tiles, axis=0).astype(jnp.bfloat16)

    mine = z * 2 + c
    share = 2 * nz // chunks

    def line(i):
        return (i // 2 * 4 + y * 2 + lax.rem(i, 2), t)

    def send_columns(j):
        @pl.when(mine != j * share)
        def _():
            remote(colbuf.at[j], colin.at[mine], ksend.at[0], krecv.at[0], line(j * share)).start()

        @pl.when(mine == j * share)
        def _():
            colin[mine] = colbuf[j]

    owns = jnp.logical_and(lax.rem(mine, share) == 0, mine < last * share)

    def knn_of(ref):
        best = absorb(lowest((4 * lanes, 128)), [ref[p].astype(jnp.float32) for p in range(ns)])
        mean = mean_of(fold_sublanes(best, (2, 1)))
        return jnp.concatenate([mean[4 * q + 3 : 4 * q + 4] for q in range(lanes)], axis=0)

    def line_copy():
        return remote(lineown, linein, osend.at[0], orecv.at[0], over)

    def mean_copy(k):
        return remote(ktown, kt_out.at[mine // share], msend.at[0], mrecv.at[0], line(lax.rem(mine + k, 2 * nz)))

    def merge_line():
        @pl.when(owns)
        def _():
            ref = colin.at[pl.ds(0, 2 * nz - 1)]
            remote(ref, ref, ksend.at[0], krecv.at[0], core).wait_recv()
            best = absorb(lowest((4 * lanes, 128)), [colin[p].astype(jnp.float32) for p in range(2 * nz)])
            best = fold_sublanes(best, (2, 1))
            row = lax.rem(lax.broadcasted_iota(jnp.int32, (4 * lanes, 128), 0), 4)
            out = best[3]
            for k in range(3):
                out = jnp.where(row == k, pltpu.roll(best[k], 4 * lanes - 3 + k, 0), out)
            lineown[...] = out.astype(jnp.bfloat16)
            line_copy().start()

    def merge_columns():
        @pl.when(owns)
        def _():
            line_copy().wait_recv()
            ours, theirs = lineown[...].astype(jnp.float32), linein[...].astype(jnp.float32)
            best = fold_sublanes(insert(insert(lowest((4 * lanes, 128)), ours), theirs), (2, 1))
            mean = mean_of(best)
            ktown[...] = jnp.concatenate([mean[4 * q + 3 : 4 * q + 4] for q in range(lanes)], axis=0)
            for k in range(1, 2 * nz):
                mean_copy(k).start()
            kt_out[mine // share] = ktown[...]

    def within(j):
        return jnp.logical_and(j >= 0, j < first)

    def relay(to_side, there, behind_me, j):
        for d in range(1, nz):
            zp, present = behind_me(d)

            @pl.when(present)
            def _():
                to_side(j, zp).wait_recv()

                to_over(j, zp).start()

                @pl.when(there)
                def _():
                    to_side(j, zp).start()

    relays = (
        functools.partial(relay, to_left, has_left, lambda d: (z + d, z + d < nz)),
        functools.partial(relay, to_right, has_right, lambda d: (z - d, z - d >= 0)),
    )

    sides_both = (
        (both_left, has_left, HOP * z - depth, lambda d: (z + d, z + d < nz)),
        (both_right, has_right, -HOP * z, lambda d: (z - d, z - d >= 0)),
    )

    y_behind = depth + Y_LAG
    behind = y_behind + CORE_LAG

    def for_peers(what):
        for q in range(nz):
            zz = jnp.where(z < nz // 2, nz - 1 - q, q)
            for a in (1, 0):
                for b in (1, 0):
                    to = zz * 4 + lax.rem(y + a, 2) * 2 + lax.rem(c + b, 2)
                    if a or b:
                        what(to)
                    else:
                        pl.when(zz != z)(functools.partial(what, to))

    def tail_copy(e, to):
        src = colbuf.at[first - e]
        return remote(src, tailin.at[e, s], tsend.at[0], trecv.at[e], (to, t))

    def y_done(j):
        from_over(j).wait_recv()
        to_core(j, 1 - y).start()

    def tick(i, carry):
        for (to_side, there, lead), relay_side in zip(sides, relays):
            j = i + lead

            @pl.when(jnp.logical_and(within(j + z_ahead), there))
            def _():
                to_side(j + z_ahead, z, True).start()

            @pl.when(within(j))
            def _():
                relay_side(j)

        j = i - depth

        @pl.when(jnp.logical_and(j >= 0, j + y_ahead < first))
        def _():
            to_over(j + y_ahead, z, True).start()

        @pl.when(within(j))
        def _():
            to_core(j, y).start()

        m = i - behind
        jc = jnp.where(m == last, first, jnp.where(m == first, last, m))

        @pl.when(m == NORM_AT)
        def _():
            normalize_sources()

        @pl.when(m == last)
        def _():
            for which, slot in ((near, last), (pl.ds(far, 1), chunks)):
                ref = g.at[last, which, 1 - y, c]
                remote(ref, ref, ysend.at[0], yrecv.at[slot], over).wait_recv()
                ref = g.at[last, which, 1 - y, c]
                remote(ref, ref, csend.at[0], crecv.at[last], core).start()
            merge_line()

        @pl.when(m >= 0)
        def _():
            from_core(jc).wait_recv()
            compute(jc)


        @pl.when(jnp.logical_and(m >= 0, m < last))
        def _():
            send_columns(jc)

        @pl.when(m >= last)
        def _():
            for_peers(lambda to: tail_copy(m - last, to).start())
            tailin[m - last, s] = colbuf[jc]

        for both, there, lead, behind_me in sides_both:

            @pl.when(jnp.logical_and(i == first - lead - FIRST_LEAD, there))
            def _():
                both(z).start()

        final = last - 1 + behind
        for d in range(1, nz):
            for both, there, lead, behind_me in sides_both:
                zp, present = behind_me(d)
                at = jnp.where(there, jnp.minimum(first - lead + FIRST_GAP * (d - 1), final), final)

                @pl.when(jnp.logical_and(present, i == at))
                def _():
                    both(zp).wait_recv()

                    @pl.when(there)
                    def _():
                        both(zp).start()

        @pl.when(i == final)
        def _():
            to_core(first, y).start()
            to_core(first, 1 - y).start()

        jy = i - y_behind

        @pl.when(jnp.logical_and(jy >= 0, jy < last))
        def _():
            y_done(jy)

        return carry

    lax.fori_loop(0, chunks + behind, tick, 0)

    def row_copy(k):
        return remote(rowbuf, rowin.at[t], rsend.at[0], rrecv.at[0], (s, lax.rem(t + k, nt)))

    flat = [rowbest[k].T for k in range(4)]
    best = lowest((8, rows))
    for q in range(128 // 8):
        best = merge(best, tuple(flat[k][q * 8 : (q + 1) * 8, :] for k in range(4)))
    best = fold_sublanes(best)
    row = lax.broadcasted_iota(jnp.int32, (8, rows), 0)
    out = jnp.full((8, rows), -jnp.inf, jnp.float32)
    for k in range(4):
        out = jnp.where(row == k, best[k], out)
    rowbuf[...] = out
    rowin[t] = out
    for k in range(1, nt):
        row_copy(k).start()
    merge_columns()

    def drain_z(side, where, count):
        for kind, ref in enumerate((g.at[pl.ds(0, first), pl.ds(0, count), 0, 0], g.at[0, pl.ds(0, count), :, 0])):
            remote(ref, ref, zsend.at[side, kind], zrecv.at[0, 0], where).wait_send()

    for zz in range(nz):

        @pl.when(z == zz)
        def _():
            if zz + 1 < nz:
                drain_z(0, right, zz + 1)
            if zz >= 1:
                drain_z(1, left, nz - zz)

    ref = g.at[pl.ds(0, first), :, 0, 0]
    remote(ref, ref, ysend.at[0], yrecv.at[0], over).wait_send()
    swap(True).wait_send()
    ref = g.at[:, :, :, c]
    remote(ref, ref, csend.at[0], crecv.at[0], core).wait_send()
    for k in range(1, nt):
        to_tgt(k).wait_send()

    def tail_done(e):
        ref = tailin.at[e, pl.ds(0, ns - 1)]
        remote(ref, ref, tsend.at[0], trecv.at[e], core).wait_recv()
        kt_out[first - e] = knn_of(tailin.at[e])

    tail_done(0)
    for k in range(1, nt):
        row_copy(k).wait_send()
    ref = rowin.at[pl.ds(0, nt - 1)]
    remote(ref, ref, rsend.at[0], rrecv.at[0], core).wait_recv()
    half = 0.5 * mean_of(fold_sublanes(absorb(lowest((8, rows)), [rowin[p] for p in range(nt)])))
    ks_out[...] = jnp.broadcast_to(half[0:1], (128, rows)).T
    tail_done(1)
    @pl.when(owns)
    def _():
        ref = colbuf.at[pl.ds(0, last - 1)]
        remote(ref, ref, ksend.at[0], krecv.at[0], core).wait_send()
        mean = kt_out.at[pl.ds(0, last - 1)]
        remote(mean, mean, msend.at[0], mrecv.at[0], core).wait_recv()
        for k in range(1, 2 * nz):
            mean_copy(k).wait_send()
        line_copy().wait_send()

    @pl.when(jnp.logical_not(owns))
    def _():
        ref = colbuf.at[pl.ds(0, last)]
        remote(ref, ref, ksend.at[0], krecv.at[0], core).wait_send()
        mean = kt_out.at[pl.ds(0, last)]
        remote(mean, mean, msend.at[0], mrecv.at[0], core).wait_recv()

    ref = tailin.at[:, pl.ds(0, ns - 1)]
    remote(ref, ref, tsend.at[0], trecv.at[0], core).wait_send()


def finish(s_ref, kt_ref, ks_ref, out_ref, half, held, sem):
    rows, cols = s_ref.shape
    tiles = cols // 128
    lanes = kt_ref.shape[1]
    for j in range(tiles):
        half[j] = jnp.broadcast_to(0.5 * kt_ref[j // lanes, j % lanes : j % lanes + 1, :], (8, 128))

    def block(b, carry):
        def at(h):
            return pl.ds(pl.multiple_of(b * BLOCK + 8 * h, 8), 8)

        mine = [ks_ref[at(h), :] for h in range(BLOCK // 8)]
        for q in range(tiles):
            lanes = slice(q * 128, (q + 1) * 128)
            other = half[q]
            for h in range(BLOCK // 8):
                v = s_ref[at(h), lanes]
                held[at(h), lanes] = jnp.where(v == excluded_score, jnp.float32(0.0), v / (mine[h] + other))
        span = pl.ds(pl.multiple_of(b * BLOCK, BLOCK), BLOCK)
        pltpu.make_async_copy(held.at[span], out_ref.at[span], sem.at[0]).start()
        return carry

    lax.fori_loop(0, rows // BLOCK, block, 0)
    pltpu.make_async_copy(held, out_ref, sem.at[0]).wait()


def body(ns, nt, src_emb, tgt_emb, src_ids, tgt_ids):
    rows, part = src_emb.shape
    cols, feats = tgt_emb.shape
    width = part * nt
    nz = ns // 4
    cw = min(CHUNK, cols)
    chunks = cols // cw
    lanes = cw // 128
    f32, bf16 = jnp.float32, jnp.bfloat16
    dma = pltpu.SemaphoreType.DMA
    hbm = pl.BlockSpec(memory_space=pltpu.MemorySpace.HBM)
    vmem = pl.BlockSpec(memory_space=pltpu.VMEM)
    args = (tgt_emb.T, src_emb, src_ids.reshape(1, rows), tgt_ids.reshape(1, cols))
    scores, kt, ks = pl.pallas_call(
        functools.partial(kernel, (ns, nt, nz, chunks, cw, feats)),
        out_shape=(
            jax.ShapeDtypeStruct((rows, cols), f32),
            jax.ShapeDtypeStruct((chunks, lanes, 128), f32),
            jax.ShapeDtypeStruct((rows, 128), f32),
        ),
        in_specs=[hbm, hbm, hbm, hbm],
        out_specs=(vmem, vmem, vmem),
        scratch_shapes=[
            pltpu.VMEM((1, rows), jnp.int32),
            pltpu.VMEM((1, cols), jnp.int32),
            pltpu.VMEM((rows, 128), jnp.int32),
            pltpu.VMEM((chunks, nz, 2, 2, feats, cw), bf16),
            pltpu.VMEM((rows, width), bf16),
            pltpu.VMEM((rows, width), bf16),
            pltpu.VMEM((rows, cw), f32),
            pltpu.VMEM((4, rows, 128), f32),
            pltpu.VMEM((chunks, 4 * lanes, 128), bf16),
            pltpu.VMEM((ns, 4 * lanes, 128), bf16),
            pltpu.VMEM((2, ns, 4 * lanes, 128), bf16),
            pltpu.VMEM((4 * lanes, 128), bf16),
            pltpu.VMEM((4 * lanes, 128), bf16),
            pltpu.VMEM((lanes, 128), f32),
            pltpu.VMEM((8, rows), f32),
            pltpu.VMEM((nt, 8, rows), f32),
            dma((chunks, nz)),
            dma((2, 2)),
            dma((chunks + 1,)),
            dma((2,)),
            dma((chunks,)),
            dma((1,)),
            dma((nt,)),
            dma((1,)),
            dma((1,)),
            dma((1,)),
            dma((1,)),
            dma((1,)),
            dma((1,)),
            dma((1,)),
            dma((2,)),
            dma((1,)),
            dma((1,)),
            dma((1,)),
            dma((4,)),
        ],
        compiler_params=pltpu.CompilerParams(
            collective_id=0, has_side_effects=True, vmem_limit_bytes=40 * 2**20
        ),
    )(*(pltpu.with_memory_space_constraint(v, pltpu.MemorySpace.HBM) for v in args))
    return pl.pallas_call(
        finish,
        out_shape=jax.ShapeDtypeStruct((rows, cols), f32),
        in_specs=[vmem, vmem, vmem],
        out_specs=pl.BlockSpec(memory_space=pl.ANY),
        scratch_shapes=[
            pltpu.VMEM((cols // 128, 8, 128), f32),
            pltpu.VMEM((rows, cols), f32),
            dma((1,)),
        ],
        compiler_params=pltpu.CompilerParams(vmem_limit_bytes=40 * 2**20),
    )(scores, kt, ks)


def solution(mesh):
    return jax.shard_map(
        functools.partial(body, mesh.shape["src"], mesh.shape["tgt"]),
        mesh=mesh,
        in_specs=(P("src", "tgt"), P("tgt", "src"), P("src"), P("tgt")),
        out_specs=P("src", "tgt"),
        check_vma=False,
    )
```

```python
import functools

import jax
import jax.numpy as jnp
from jax import lax
from jax.experimental import pallas as pl
from jax.experimental.pallas import tpu as pltpu
from jax.sharding import PartitionSpec as P

epsilon = 1e-06
excluded_score = -2.0
MESH = pl.DeviceIdType.MESH
CHUNK = 512
FIRST_LEAD = 1
FIRST_GAP = 1
Z_AHEAD = 3
Y_AHEAD = 7
BLOCK = 32
HOP = 1
Y_LAG = 2
CORE_LAG = 1
NORM_AT = -1


def sort4(v):
    a, b = jnp.maximum(v[0], v[1]), jnp.minimum(v[0], v[1])
    c, d = jnp.maximum(v[2], v[3]), jnp.minimum(v[2], v[3])
    top, e = jnp.maximum(a, c), jnp.minimum(a, c)
    f, low = jnp.maximum(b, d), jnp.minimum(b, d)
    return (top, jnp.maximum(e, f), jnp.minimum(e, f), low)


def merge(first, second):
    c = [jnp.maximum(first[k], second[3 - k]) for k in range(4)]
    a, b = jnp.maximum(c[0], c[2]), jnp.maximum(c[1], c[3])
    d, e = jnp.minimum(c[0], c[2]), jnp.minimum(c[1], c[3])
    return (jnp.maximum(a, b), jnp.minimum(a, b), jnp.maximum(d, e), jnp.minimum(d, e))


def insert(best, value):
    out = []
    for level in best[:-1]:
        out.append(jnp.maximum(level, value))
        value = jnp.minimum(level, value)
    out.append(jnp.maximum(best[-1], value))
    return tuple(out)


def absorb(best, values):
    whole = len(values) // 4 * 4
    for k in range(0, whole, 4):
        best = merge(best, sort4(values[k : k + 4]))
    for value in values[whole:]:
        best = insert(best, value)
    return best


def fold_sublanes(best, shifts=(4, 2, 1)):
    for shift in shifts:
        best = merge(best, tuple(pltpu.roll(level, shift, 0) for level in best))
    return best


def mean_of(best):
    return (best[0] + best[1] + best[2] + best[3]) * 0.25


def lowest(shape):
    return tuple(jnp.full(shape, -jnp.inf, jnp.float32) for _ in range(4))


def kernel(dims, x_ref, a_ref, sid_ref, tid_ref, s_out, kt_out, ks_out, sid, tid, sids, g, a_whole, a_unit, raw, rowbest,
           colbuf, colin, tailin, lineown, linein, ktown, rowbuf, rowin, zrecv, zsend, yrecv, ysend, crecv, csend, arecv, asend, rrecv,
           rsend, krecv, ksend, mrecv, msend, trecv, tsend, osend, orecv, lsem):
    ns, nt, nz, chunks, cw, feats = dims
    s = lax.axis_index("src")
    t = lax.axis_index("tgt")
    z, y, c = s // 4, (s // 2) % 2, s % 2
    right = (s + 4, t)
    left = (s - 4, t)
    over = (z * 4 + (1 - y) * 2 + c, t)
    core = (s + 1 - 2 * c, t)
    rows, width = a_unit.shape
    part = a_ref.shape[1]
    lanes = cw // 128
    first = chunks - 1
    last = first - 1
    has_right, has_left = z + 1 < nz, z >= 1

    def remote(src, dst, send, recv, where):
        return pltpu.make_async_remote_copy(
            src_ref=src, dst_ref=dst, send_sem=send, recv_sem=recv, device_id=where, device_id_type=MESH
        )

    def chunk_cols(j):
        return pl.ds(pl.multiple_of(j * cw, cw), cw)

    barrier = pltpu.get_barrier_semaphore()

    @pl.when(has_right)
    def _():
        pl.semaphore_signal(barrier, inc=1, device_id=right, device_id_type=MESH)

    @pl.when(has_left)
    def _():
        pl.semaphore_signal(barrier, inc=1, device_id=left, device_id_type=MESH)

    pl.semaphore_signal(barrier, inc=1, device_id=over, device_id_type=MESH)
    pl.semaphore_signal(barrier, inc=1, device_id=core, device_id_type=MESH)
    for k in range(1, nt):
        pl.semaphore_signal(barrier, inc=1, device_id=(s, lax.rem(t + k, nt)), device_id_type=MESH)

    for j in range(chunks):
        pltpu.make_async_copy(x_ref.at[:, chunk_cols(j)], g.at[j, z, y, c], lsem.at[0]).start()
    acols = pl.ds(pl.multiple_of(t * part, part), part)
    local_a = pltpu.make_async_copy(a_ref, a_whole.at[:, acols], lsem.at[1])
    local_sid = pltpu.make_async_copy(sid_ref, sid, lsem.at[2])
    local_tid = pltpu.make_async_copy(tid_ref, tid, lsem.at[3])
    local_a.start()
    local_sid.start()
    local_tid.start()
    pl.semaphore_wait(barrier, 1 + nt + has_right.astype(jnp.int32) + has_left.astype(jnp.int32))

    def to_right(j, zp, own=False):
        ref = g.at[j, zp, y, c]
        return remote(x_ref.at[:, chunk_cols(j)] if own else ref, ref, zsend.at[0, 0], zrecv.at[j, zp], right)

    def to_left(j, zp, own=False):
        ref = g.at[j, zp, y, c]
        return remote(x_ref.at[:, chunk_cols(j)] if own else ref, ref, zsend.at[1, 0], zrecv.at[j, zp], left)

    def both_right(zp):
        ref = g.at[first, zp, :, c]
        return remote(ref, ref, zsend.at[0, 1], zrecv.at[first, zp], right)

    def both_left(zp):
        ref = g.at[first, zp, :, c]
        return remote(ref, ref, zsend.at[1, 1], zrecv.at[first, zp], left)

    far = jnp.where(z < nz // 2, nz - 1, 0)
    near = pl.ds(jnp.where(z < nz // 2, 0, 1), nz - 1)

    def to_over(j, zp, own=False):
        ref = g.at[j, zp, y, c]
        src = x_ref.at[:, chunk_cols(j)] if own else ref
        slot = jnp.where(jnp.logical_and(j == last, zp == far), chunks, j)
        return remote(src, ref, ysend.at[0], yrecv.at[slot], over)

    def from_over(j):
        ref = g.at[j, :, 1 - y, c]
        return remote(ref, ref, ysend.at[0], yrecv.at[j], over)

    def swap(own):
        ref = g.at[first, z, y, c] if own else g.at[first, z, 1 - y, c]
        return remote(x_ref.at[:, chunk_cols(first)] if own else ref, ref, ysend.at[1], yrecv.at[first], over)

    def to_core(j, yy):
        ref = g.at[j, :, yy, c]
        return remote(ref, ref, csend.at[0], crecv.at[j], core)

    def from_core(j):
        ref = g.at[j, :, :, 1 - c]
        return remote(ref, ref, csend.at[0], crecv.at[j], core)

    def to_tgt(k):
        return remote(a_ref, a_whole.at[:, acols], asend.at[0], arecv.at[t], (s, lax.rem(t + k, nt)))

    z_ahead, y_ahead = min(Z_AHEAD, first - 1), min(Y_AHEAD, first)
    depth = HOP * (nz - 1)
    sides = ((to_left, has_left, HOP * z - depth), (to_right, has_right, -HOP * z))
    swap(True).start()
    for j in range(max(y_ahead, z_ahead)):
        if j < y_ahead:
            to_over(j, z, True).start()
        if j < z_ahead:
            for to_side, there, lead in sides:

                @pl.when(jnp.logical_and(there, j < lead + z_ahead))
                def _():
                    to_side(j, z, True).start()

    for k in range(1, nt):
        to_tgt(k).start()
    pltpu.make_async_copy(g.at[:, z, y, c], g.at[:, z, y, c], lsem.at[0]).wait()
    swap(False).wait_recv()
    local_sid.wait()
    local_tid.wait()
    sids[...] = jnp.broadcast_to(sid[...], (128, rows)).T
    for k in range(4):
        rowbest[k] = jnp.full(rowbest.shape[1:], -jnp.inf, jnp.float32)

    def normalize_sources():
        local_a.wait()
        for k in range(1, nt):
            other = lax.rem(t + k, nt)
            cols = pl.ds(pl.multiple_of(other * part, part), part)
            remote(a_ref, a_whole.at[:, cols], asend.at[0], arecv.at[other], (s, other)).wait_recv()
        block = 16

        def step(r, carry):
            at = pl.ds(pl.multiple_of(r * block, block), block)
            v = a_whole[at, :].astype(jnp.float32)
            scale = jnp.sqrt(jnp.sum(v * v, axis=1, keepdims=True) + epsilon)
            a_unit[at, :] = (v / scale).astype(jnp.bfloat16)
            return carry

        lax.fori_loop(0, rows // block, step, 0, unroll=2)

    def compute(j):
        cols = chunk_cols(j)
        found = g[j].reshape(width, cw)
        raw[...] = jnp.dot(a_unit[...], found, preferred_element_type=jnp.float32)
        found = found.astype(jnp.float32)
        acc = jnp.sum((found * found).reshape(width // 8, 8, cw), axis=0)
        inverse = jnp.broadcast_to(1.0 / jnp.sqrt(jnp.sum(acc, axis=0, keepdims=True) + epsilon), (8, cw))
        tids = jnp.broadcast_to(tid[:, cols], (8, cw))

        def group(r, best):
            ats = [pl.ds(pl.multiple_of(r * 32 + h * 8, 8), 8) for h in range(4)]
            spans = [slice(q * 128, (q + 1) * 128) for q in range(lanes)]
            ids = [sids[at, :] for at in ats]
            found = [[raw[at, span] for span in spans] for at in ats]
            rows_in = [tuple(rowbest[k, at, :] for k in range(4)) for at in ats]
            found = [
                [jnp.where(ids[h] == tids[:, span], jnp.float32(excluded_score), v * inverse[:, span]) for v, span in zip(found[h], spans)]
                for h in range(4)
            ]
            rows_out = [absorb(rows_in[h], found[h]) for h in range(4)]
            best = tuple(absorb(best[q], [found[h][q] for h in range(4)]) for q in range(lanes))
            for h, at in enumerate(ats):
                for q in range(lanes):
                    s_out[at, pl.ds(pl.multiple_of(j * cw + q * 128, 128), 128)] = found[h][q]
                for k in range(4):
                    rowbest[k, at, :] = rows_out[h][k]
            return best

        best = lax.fori_loop(0, rows // 32, group, tuple(lowest((8, 128)) for _ in range(lanes)), unroll=2)
        best = [fold_sublanes(b) for b in best]
        row = lax.broadcasted_iota(jnp.int32, (8, 128), 0)
        tiles = []
        for q in range(0, lanes, 2):
            out = best[q][0]
            for k in range(1, 8):
                out = jnp.where(row == k, best[q + k // 4][k % 4], out)
            tiles.append(out)
        colbuf[j] = jnp.concatenate(tiles, axis=0).astype(jnp.bfloat16)

    mine = z * 2 + c
    share = 2 * nz // chunks

    def line(i):
        return (i // 2 * 4 + y * 2 + lax.rem(i, 2), t)

    def send_columns(j):
        @pl.when(mine != j * share)
        def _():
            remote(colbuf.at[j], colin.at[mine], ksend.at[0], krecv.at[0], line(j * share)).start()

        @pl.when(mine == j * share)
        def _():
            colin[mine] = colbuf[j]

    owns = jnp.logical_and(lax.rem(mine, share) == 0, mine < last * share)

    def knn_of(ref):
        best = absorb(lowest((4 * lanes, 128)), [ref[p].astype(jnp.float32) for p in range(ns)])
        mean = mean_of(fold_sublanes(best, (2, 1)))
        return jnp.concatenate([mean[4 * q + 3 : 4 * q + 4] for q in range(lanes)], axis=0)

    def line_copy():
        return remote(lineown, linein, osend.at[0], orecv.at[0], over)

    def mean_copy(k):
        return remote(ktown, kt_out.at[mine // share], msend.at[0], mrecv.at[0], line(lax.rem(mine + k, 2 * nz)))

    def merge_line():
        @pl.when(owns)
        def _():
            ref = colin.at[pl.ds(0, 2 * nz - 1)]
            remote(ref, ref, ksend.at[0], krecv.at[0], core).wait_recv()
            best = absorb(lowest((4 * lanes, 128)), [colin[p].astype(jnp.float32) for p in range(2 * nz)])
            best = fold_sublanes(best, (2, 1))
            row = lax.rem(lax.broadcasted_iota(jnp.int32, (4 * lanes, 128), 0), 4)
            out = best[3]
            for k in range(3):
                out = jnp.where(row == k, pltpu.roll(best[k], 4 * lanes - 3 + k, 0), out)
            lineown[...] = out.astype(jnp.bfloat16)
            line_copy().start()

    def merge_columns():
        @pl.when(owns)
        def _():
            line_copy().wait_recv()
            ours, theirs = lineown[...].astype(jnp.float32), linein[...].astype(jnp.float32)
            best = fold_sublanes(insert(insert(lowest((4 * lanes, 128)), ours), theirs), (2, 1))
            mean = mean_of(best)
            ktown[...] = jnp.concatenate([mean[4 * q + 3 : 4 * q + 4] for q in range(lanes)], axis=0)
            for k in range(1, 2 * nz):
                mean_copy(k).start()
            kt_out[mine // share] = ktown[...]

    def within(j):
        return jnp.logical_and(j >= 0, j < first)

    def relay(to_side, there, behind_me, j):
        for d in range(1, nz):
            zp, present = behind_me(d)

            @pl.when(present)
            def _():
                to_side(j, zp).wait_recv()

                to_over(j, zp).start()

                @pl.when(there)
                def _():
                    to_side(j, zp).start()

    relays = (
        functools.partial(relay, to_left, has_left, lambda d: (z + d, z + d < nz)),
        functools.partial(relay, to_right, has_right, lambda d: (z - d, z - d >= 0)),
    )

    sides_both = (
        (both_left, has_left, HOP * z - depth, lambda d: (z + d, z + d < nz)),
        (both_right, has_right, -HOP * z, lambda d: (z - d, z - d >= 0)),
    )

    y_behind = depth + Y_LAG
    behind = y_behind + CORE_LAG

    def for_peers(what):
        for q in range(nz):
            zz = jnp.where(z < nz // 2, nz - 1 - q, q)
            for a in (1, 0):
                for b in (1, 0):
                    to = zz * 4 + lax.rem(y + a, 2) * 2 + lax.rem(c + b, 2)
                    if a or b:
                        what(to)
                    else:
                        pl.when(zz != z)(functools.partial(what, to))

    def tail_copy(e, to):
        src = colbuf.at[first - e]
        return remote(src, tailin.at[e, s], tsend.at[0], trecv.at[e], (to, t))

    def y_done(j):
        from_over(j).wait_recv()
        to_core(j, 1 - y).start()

    def tick(i, carry):
        for (to_side, there, lead), relay_side in zip(sides, relays):
            j = i + lead

            @pl.when(jnp.logical_and(within(j + z_ahead), there))
            def _():
                to_side(j + z_ahead, z, True).start()

            @pl.when(within(j))
            def _():
                relay_side(j)

        j = i - depth

        @pl.when(jnp.logical_and(j >= 0, j + y_ahead < first))
        def _():
            to_over(j + y_ahead, z, True).start()

        @pl.when(within(j))
        def _():
            to_core(j, y).start()

        m = i - behind
        jc = jnp.where(m == last, first, jnp.where(m == first, last, m))

        @pl.when(m == NORM_AT)
        def _():
            normalize_sources()

        @pl.when(m == last)
        def _():
            for which, slot in ((near, last), (pl.ds(far, 1), chunks)):
                ref = g.at[last, which, 1 - y, c]
                remote(ref, ref, ysend.at[0], yrecv.at[slot], over).wait_recv()
                ref = g.at[last, which, 1 - y, c]
                remote(ref, ref, csend.at[0], crecv.at[last], core).start()
            merge_line()

        @pl.when(m >= 0)
        def _():
            from_core(jc).wait_recv()
            compute(jc)


        @pl.when(jnp.logical_and(m >= 0, m < last))
        def _():
            send_columns(jc)

        @pl.when(m >= last)
        def _():
            for_peers(lambda to: tail_copy(m - last, to).start())
            tailin[m - last, s] = colbuf[jc]

        for both, there, lead, behind_me in sides_both:

            @pl.when(jnp.logical_and(i == first - lead - FIRST_LEAD, there))
            def _():
                both(z).start()

        final = last - 1 + behind
        for d in range(1, nz):
            for both, there, lead, behind_me in sides_both:
                zp, present = behind_me(d)
                at = jnp.where(there, jnp.minimum(first - lead + FIRST_GAP * (d - 1), final), final)

                @pl.when(jnp.logical_and(present, i == at))
                def _():
                    both(zp).wait_recv()

                    @pl.when(there)
                    def _():
                        both(zp).start()

        @pl.when(i == final)
        def _():
            to_core(first, y).start()
            to_core(first, 1 - y).start()

        jy = i - y_behind

        @pl.when(jnp.logical_and(jy >= 0, jy < last))
        def _():
            y_done(jy)

        return carry

    lax.fori_loop(0, chunks + behind, tick, 0)

    def row_copy(k):
        return remote(rowbuf, rowin.at[t], rsend.at[0], rrecv.at[0], (s, lax.rem(t + k, nt)))

    merge_columns()
    flat = [rowbest[k].T for k in range(4)]
    best = lowest((8, rows))
    for q in range(128 // 8):
        best = merge(best, tuple(flat[k][q * 8 : (q + 1) * 8, :] for k in range(4)))
    best = fold_sublanes(best)
    row = lax.broadcasted_iota(jnp.int32, (8, rows), 0)
    out = jnp.full((8, rows), -jnp.inf, jnp.float32)
    for k in range(4):
        out = jnp.where(row == k, best[k], out)
    rowbuf[...] = out
    rowin[t] = out
    for k in range(1, nt):
        row_copy(k).start()

    def drain_z(side, where, count):
        for kind, ref in enumerate((g.at[pl.ds(0, first), pl.ds(0, count), 0, 0], g.at[0, pl.ds(0, count), :, 0])):
            remote(ref, ref, zsend.at[side, kind], zrecv.at[0, 0], where).wait_send()

    for zz in range(nz):

        @pl.when(z == zz)
        def _():
            if zz + 1 < nz:
                drain_z(0, right, zz + 1)
            if zz >= 1:
                drain_z(1, left, nz - zz)

    ref = g.at[pl.ds(0, first), :, 0, 0]
    remote(ref, ref, ysend.at[0], yrecv.at[0], over).wait_send()
    swap(True).wait_send()
    ref = g.at[:, :, :, c]
    remote(ref, ref, csend.at[0], crecv.at[0], core).wait_send()
    for k in range(1, nt):
        to_tgt(k).wait_send()

    def tail_done(e):
        ref = tailin.at[e, pl.ds(0, ns - 1)]
        remote(ref, ref, tsend.at[0], trecv.at[e], core).wait_recv()
        kt_out[first - e] = knn_of(tailin.at[e])

    tail_done(0)
    for k in range(1, nt):
        row_copy(k).wait_send()
    ref = rowin.at[pl.ds(0, nt - 1)]
    remote(ref, ref, rsend.at[0], rrecv.at[0], core).wait_recv()
    half = 0.5 * mean_of(fold_sublanes(absorb(lowest((8, rows)), [rowin[p] for p in range(nt)])))
    ks_out[...] = jnp.broadcast_to(half[0:1], (128, rows)).T
    tail_done(1)
    @pl.when(owns)
    def _():
        ref = colbuf.at[pl.ds(0, last - 1)]
        remote(ref, ref, ksend.at[0], krecv.at[0], core).wait_send()
        mean = kt_out.at[pl.ds(0, last - 1)]
        remote(mean, mean, msend.at[0], mrecv.at[0], core).wait_recv()
        for k in range(1, 2 * nz):
            mean_copy(k).wait_send()
        line_copy().wait_send()

    @pl.when(jnp.logical_not(owns))
    def _():
        ref = colbuf.at[pl.ds(0, last)]
        remote(ref, ref, ksend.at[0], krecv.at[0], core).wait_send()
        mean = kt_out.at[pl.ds(0, last)]
        remote(mean, mean, msend.at[0], mrecv.at[0], core).wait_recv()

    ref = tailin.at[:, pl.ds(0, ns - 1)]
    remote(ref, ref, tsend.at[0], trecv.at[0], core).wait_send()


def finish(s_ref, kt_ref, ks_ref, out_ref, half, held, sem):
    rows, cols = s_ref.shape
    tiles = cols // 128
    lanes = kt_ref.shape[1]
    for j in range(tiles):
        half[j] = jnp.broadcast_to(0.5 * kt_ref[j // lanes, j % lanes : j % lanes + 1, :], (8, 128))

    def block(b, carry):
        def at(h):
            return pl.ds(pl.multiple_of(b * BLOCK + 8 * h, 8), 8)

        mine = [ks_ref[at(h), :] for h in range(BLOCK // 8)]
        for q in range(tiles):
            lanes = slice(q * 128, (q + 1) * 128)
            other = half[q]
            for h in range(BLOCK // 8):
                v = s_ref[at(h), lanes]
                held[at(h), lanes] = jnp.where(v == excluded_score, jnp.float32(0.0), v / (mine[h] + other))
        span = pl.ds(pl.multiple_of(b * BLOCK, BLOCK), BLOCK)
        pltpu.make_async_copy(held.at[span], out_ref.at[span], sem.at[0]).start()
        return carry

    lax.fori_loop(0, rows // BLOCK, block, 0)
    pltpu.make_async_copy(held, out_ref, sem.at[0]).wait()


def body(ns, nt, src_emb, tgt_emb, src_ids, tgt_ids):
    rows, part = src_emb.shape
    cols, feats = tgt_emb.shape
    width = part * nt
    nz = ns // 4
    cw = min(CHUNK, cols)
    chunks = cols // cw
    lanes = cw // 128
    f32, bf16 = jnp.float32, jnp.bfloat16
    dma = pltpu.SemaphoreType.DMA
    hbm = pl.BlockSpec(memory_space=pltpu.MemorySpace.HBM)
    vmem = pl.BlockSpec(memory_space=pltpu.VMEM)
    args = (tgt_emb.T, src_emb, src_ids.reshape(1, rows), tgt_ids.reshape(1, cols))
    scores, kt, ks = pl.pallas_call(
        functools.partial(kernel, (ns, nt, nz, chunks, cw, feats)),
        out_shape=(
            jax.ShapeDtypeStruct((rows, cols), f32),
            jax.ShapeDtypeStruct((chunks, lanes, 128), f32),
            jax.ShapeDtypeStruct((rows, 128), f32),
        ),
        in_specs=[hbm, hbm, hbm, hbm],
        out_specs=(vmem, vmem, vmem),
        scratch_shapes=[
            pltpu.VMEM((1, rows), jnp.int32),
            pltpu.VMEM((1, cols), jnp.int32),
            pltpu.VMEM((rows, 128), jnp.int32),
            pltpu.VMEM((chunks, nz, 2, 2, feats, cw), bf16),
            pltpu.VMEM((rows, width), bf16),
            pltpu.VMEM((rows, width), bf16),
            pltpu.VMEM((rows, cw), f32),
            pltpu.VMEM((4, rows, 128), f32),
            pltpu.VMEM((chunks, 4 * lanes, 128), bf16),
            pltpu.VMEM((ns, 4 * lanes, 128), bf16),
            pltpu.VMEM((2, ns, 4 * lanes, 128), bf16),
            pltpu.VMEM((4 * lanes, 128), bf16),
            pltpu.VMEM((4 * lanes, 128), bf16),
            pltpu.VMEM((lanes, 128), f32),
            pltpu.VMEM((8, rows), f32),
            pltpu.VMEM((nt, 8, rows), f32),
            dma((chunks, nz)),
            dma((2, 2)),
            dma((chunks + 1,)),
            dma((2,)),
            dma((chunks,)),
            dma((1,)),
            dma((nt,)),
            dma((1,)),
            dma((1,)),
            dma((1,)),
            dma((1,)),
            dma((1,)),
            dma((1,)),
            dma((1,)),
            dma((2,)),
            dma((1,)),
            dma((1,)),
            dma((1,)),
            dma((4,)),
        ],
        compiler_params=pltpu.CompilerParams(
            collective_id=0, has_side_effects=True, vmem_limit_bytes=40 * 2**20
        ),
    )(*(pltpu.with_memory_space_constraint(v, pltpu.MemorySpace.HBM) for v in args))
    return pl.pallas_call(
        finish,
        out_shape=jax.ShapeDtypeStruct((rows, cols), f32),
        in_specs=[vmem, vmem, vmem],
        out_specs=pl.BlockSpec(memory_space=pl.ANY),
        scratch_shapes=[
            pltpu.VMEM((cols // 128, 8, 128), f32),
            pltpu.VMEM((rows, cols), f32),
            dma((1,)),
        ],
        compiler_params=pltpu.CompilerParams(vmem_limit_bytes=40 * 2**20),
    )(scores, kt, ks)


def solution(mesh):
    return jax.shard_map(
        functools.partial(body, mesh.shape["src"], mesh.shape["tgt"]),
        mesh=mesh,
        in_specs=(P("src", "tgt"), P("tgt", "src"), P("src"), P("tgt")),
        out_specs=P("src", "tgt"),
        check_vma=False,
    )
```
